32 devices in a mesh: lon: 16 (over z, x, core), lat: 2 (over y).
Axes of the slice: x: 2, y: 2, z: 4, core: 2. Of those that a mesh axis runs over, the one named last changes fastest.
Arguments:
- fields: bfloat16 [16, 2048, 128], P('lat', 'lon'), may hold values from -6 to 6
- cotangent: bfloat16 [16, 2048, 128], P('lat', 'lon'), may hold values from -6 to 6
- ocean_mask: int32 [2, 16], P('lat', 'lon'), may hold values from 0 to 1, as said below
- depth_kernel: float32 [7, 7, 128], replicated, may hold values from -0.875 to 0.875
- depth_bias: float32 [128], replicated, may hold values from -3 to 3
- norm_gain: float32 [128], replicated, may hold values from 0.25 to 1.75
- norm_bias: float32 [128], replicated, may hold values from -3 to 3
- weight_in: bfloat16 [128, 512], replicated, may hold values from -0.5 to 0.5
- bias_in: float32 [512], replicated, may hold values from -3 to 3
- weight_out: bfloat16 [512, 128], replicated, may hold values from -0.25 to 0.25
- bias_out: float32 [128], replicated, may hold values from -3 to 3
- layer_scale: float32 [128], replicated, may hold values from 0.3 to 1.5
Outputs:
- block_out: bfloat16 [16, 2048, 128], P('lat', 'lon')
- grad_fields: bfloat16 [16, 2048, 128], P('lat', 'lon')
- grad_mlp: float32 [2, 128, 512], P(None, 'lat', 'lon')
- grad_kernel: float32 [7, 7, 128], replicated
- grad_channels: float32 [5, 128], replicated
- grad_bias_in: float32 [512], replicated
The draws below stay inside these ranges and needn't reach their ends.
Inputs may be any that keep to these rules, and one draw needn't show every extreme that they name: `ocean_mask`: on some device every tile is ocean; on every device the tile of its first 8 rows and first 128 cells is ocean.
All inputs are finite; a program needn't handle non-finite values.
Results may differ from the reference program's by a relative error of at most 0.0057.
Values may be sent and summed in bfloat16 or wider, within the bound.
A program may use at most 64 MiB of HBM per device.

```python
import math
import jax
import jax.numpy as jnp
from jax import lax

C = 128
HID = 512
CH = 8
CW = 128
LAT = 16
LON = 2048
N_LON = 16
N_LAT = 2


def draw_ocean_mask(key, part):
    first_key, second_key, third_key = jax.random.split(key, 3)
    levels = jax.random.randint(first_key, (N_LAT, N_LON), 0, 9)
    forced = jax.random.randint(second_key, (), 0, N_LAT * N_LON)
    device_ids = jnp.arange(N_LAT * N_LON).reshape(N_LAT, N_LON)
    levels = jnp.where(device_ids == forced, 8, levels)
    ticket = jax.random.randint(third_key, (N_LAT, CH // 8, N_LON, CW // 128), 0, 8)
    ocean_tiles = (ticket < levels[:, None, :, None]).astype(jnp.int32)
    row_first = (jnp.arange(CH // 8) == 0)[None, :, None, None]
    col_first = (jnp.arange(CW // 128) == 0)[None, None, None, :]
    ocean_tiles = jnp.where(row_first & col_first, 1, ocean_tiles)
    return ocean_tiles.reshape(LAT // 8, LON // 128)


def shard_levels(key, extent, cuts, smallest, high):
    level, own = 1.0, jax.random.fold_in(key, 6)
    for dim, blocks in cuts:
        heights = jnp.exp(jax.random.uniform(jax.random.fold_in(own, dim), (blocks,), jnp.float32, smallest / len(cuts), high / len(cuts)))
        level = level * jnp.repeat(heights, extent[dim] // blocks).reshape([-1 if axis == dim else 1 for axis in range(len(extent))])
    return level


def bell_draw(own_key, shape, deviation, most, pieces=(), dtype=jnp.bfloat16):
    values = deviation * jax.random.normal(own_key, shape, jnp.float32)
    if pieces:
        values = values * shard_levels(own_key, shape, pieces, -0.22, 0.18)
    return jnp.clip(values, -most, most).astype(dtype)


def setup_inputs(seed: int = 0) -> dict:
    key_of = jax.random.split(jax.random.key(seed), 13)
    return {
        "fields": bell_draw(key_of[0], (LAT, LON, C), 1.0, 6.0, ((0, 2), (1, 16))),
        "cotangent": bell_draw(key_of[1], (LAT, LON, C), 1.0, 6.0, ((0, 2), (1, 16))),
        "ocean_mask": draw_ocean_mask(jax.random.fold_in(key_of[12], 71), 0),
        "depth_kernel": bell_draw(key_of[3], (7, 7, C), 49 ** -0.5, 0.875, (), jnp.float32),
        "depth_bias": bell_draw(key_of[4], (C,), 0.5, 3.0, (), jnp.float32),
        "norm_gain": jnp.clip(1.0 + 0.15 * jax.random.normal(key_of[5], (C,), jnp.float32), 0.25, 1.75),
        "norm_bias": bell_draw(key_of[6], (C,), 0.5, 3.0, (), jnp.float32),
        "weight_in": bell_draw(key_of[7], (C, HID), C ** -0.5, 0.5),
        "bias_in": bell_draw(key_of[8], (HID,), 0.5, 3.0, (), jnp.float32),
        "weight_out": bell_draw(key_of[9], (HID, C), HID ** -0.5, 0.25),
        "bias_out": bell_draw(key_of[10], (C,), 0.5, 3.0, (), jnp.float32),
        "layer_scale": jnp.clip(jnp.exp(jax.random.uniform(key_of[11], (C,), jnp.float32, math.log(0.3), math.log(1.5))), 0.3, 1.5),
    }


GELU_COEF = 0.7978845608028654

def gelu_pair(pre_act):
    cubic_term = 0.044715 * pre_act * pre_act * pre_act
    tanh_val = jnp.tanh(GELU_COEF * (pre_act + cubic_term))
    activated = 0.5 * pre_act * (1.0 + tanh_val)
    derivative = 0.5 * (1.0 + tanh_val) + 0.5 * pre_act * (1.0 - tanh_val * tanh_val) * GELU_COEF * (1.0 + 3.0 * 0.044715 * pre_act * pre_act)
    return (activated, derivative)

def tile_pass(depth_rows, grad_rows, ocean_weight, norm_gain, norm_bias, weight_in, bias_in, weight_out, bias_out, layer_scale):
    center_mean = lax.optimization_barrier(jnp.mean(depth_rows, axis=-1, keepdims=True))
    centered = depth_rows - center_mean
    variance = lax.optimization_barrier(jnp.mean(centered * centered, axis=-1, keepdims=True))
    inverse = lax.rsqrt(variance + 1e-06)
    normed = centered * inverse
    normed_low = (normed * norm_gain + norm_bias).astype(jnp.bfloat16)
    pre_act = jnp.dot(normed_low, weight_in, preferred_element_type=jnp.float32) + bias_in
    activated, derivative = gelu_pair(pre_act)
    hidden_low = activated.astype(jnp.bfloat16)
    output_rows = jnp.dot(hidden_low, weight_out, preferred_element_type=jnp.float32) + bias_out
    scaled = ocean_weight * layer_scale
    branch = scaled * output_rows
    grad_out = scaled * grad_rows
    grad_out_low = grad_out.astype(jnp.bfloat16)
    grad_hidden = lax.dot_general(grad_out_low, weight_out, (((1,), (1,)), ((), ())), preferred_element_type=jnp.float32)
    grad_pre = grad_hidden * derivative
    grad_pre_low = grad_pre.astype(jnp.bfloat16)
    grad_normed = lax.dot_general(grad_pre_low, weight_in, (((1,), (1,)), ((), ())), preferred_element_type=jnp.float32)
    grad_hat = grad_normed * norm_gain
    grad_depth = inverse * (grad_hat - lax.optimization_barrier(jnp.mean(grad_hat, axis=-1, keepdims=True)) - normed * lax.optimization_barrier(jnp.mean(grad_hat * normed, axis=-1, keepdims=True)))
    grad_win = lax.dot_general(normed_low, grad_pre_low, (((0,), (0,)), ((), ())), preferred_element_type=jnp.float32)
    grad_wout = lax.dot_general(grad_out_low, hidden_low, (((0,), (0,)), ((), ())), preferred_element_type=jnp.float32)
    channel_sums = jnp.stack([lax.optimization_barrier(jnp.sum(grad_depth, axis=0)), lax.optimization_barrier(jnp.sum(grad_normed * normed, axis=0)), lax.optimization_barrier(jnp.sum(grad_normed, axis=0)), lax.optimization_barrier(jnp.sum(grad_out, axis=0)), lax.optimization_barrier(jnp.sum(ocean_weight * output_rows * grad_rows, axis=0))])
    bias_sums = lax.optimization_barrier(jnp.sum(grad_pre, axis=0))
    return (branch, grad_depth, jnp.stack([grad_win, grad_wout]), channel_sums, bias_sums)

def pad_field(values):
    wrapped = jnp.concatenate([values[:, -3:], values, values[:, :3]], axis=1)
    return jnp.pad(wrapped, ((3, 3), (0, 0), (0, 0)))

def convolve(padded, depth_kernel, lat_rows, lon_cols):
    result = jnp.zeros((lat_rows, lon_cols, padded.shape[2]), jnp.float32)
    for tap_row in range(7):
        for tap_col in range(7):
            result = result + depth_kernel[tap_row, tap_col] * padded[tap_row:tap_row + lat_rows, tap_col:tap_col + lon_cols].astype(jnp.float32)
    return result

def adjoint(grad_padded, depth_kernel, lat_rows, lon_cols):
    result = jnp.zeros((lat_rows, lon_cols, grad_padded.shape[2]), jnp.float32)
    for tap_row in range(7):
        for tap_col in range(7):
            result = result + depth_kernel[tap_row, tap_col] * grad_padded[6 - tap_row:6 - tap_row + lat_rows, 6 - tap_col:6 - tap_col + lon_cols]
    return result

def kernel_terms(padded, grad_depth, lat_rows, lon_cols):
    collected = []
    for tap_row in range(7):
        for tap_col in range(7):
            collected.append(lax.optimization_barrier(jnp.sum(padded[tap_row:tap_row + lat_rows, tap_col:tap_col + lon_cols].astype(jnp.float32) * grad_depth, axis=(0, 1))))
    return jnp.stack(collected).reshape(7, 7, grad_depth.shape[2])

def reference(fields, cotangent, ocean_mask, depth_kernel, depth_bias, norm_gain, norm_bias, weight_in, bias_in, weight_out, bias_out, layer_scale):
    channels = fields.shape[2]
    padded = pad_field(fields)
    depth_out = convolve(padded, depth_kernel, LAT, LON) + depth_bias
    depth_blocks = depth_out.reshape(LAT // 8, 8 * LON, channels)
    grad_blocks = cotangent.reshape(LAT // 8, 8 * LON, channels)
    cell_mask = jnp.tile(jnp.repeat(ocean_mask, 128, axis=1), (1, 8)).astype(jnp.float32)

    def block_step(state_tuple, inputs):
        depth_rows, grad_rows, mask_rows = inputs
        branch, grad_depth, mlp_terms, chan_terms, bias_terms = tile_pass(depth_rows, grad_rows.astype(jnp.float32), mask_rows[:, None], norm_gain, norm_bias, weight_in, bias_in, weight_out, bias_out, layer_scale)
        return ((state_tuple[0] + mlp_terms, state_tuple[1] + chan_terms, state_tuple[2] + bias_terms), (branch, grad_depth))
    initial = (jnp.zeros((2, channels, weight_in.shape[1]), jnp.float32), jnp.zeros((5, channels), jnp.float32), jnp.zeros((weight_in.shape[1],), jnp.float32))
    totals, produced = lax.scan(block_step, initial, (depth_blocks, grad_blocks, cell_mask))
    branch_all = produced[0].reshape(LAT, LON, channels)
    grad_depth_all = produced[1].reshape(LAT, LON, channels)
    block_out = (fields.astype(jnp.float32) + branch_all).astype(jnp.bfloat16)
    grad_padded = pad_field(grad_depth_all)
    grad_fields = (cotangent.astype(jnp.float32) + adjoint(grad_padded, depth_kernel, LAT, LON)).astype(jnp.bfloat16)
    kernel_sum = kernel_terms(padded, grad_depth_all, LAT, LON)
    grad_scale = 1.0 / math.sqrt(LAT * LON)
    return (block_out, grad_fields, totals[0] * grad_scale, kernel_sum * grad_scale, totals[1] * grad_scale, totals[2] * grad_scale)
```

```python
import functools
import math

import jax
import jax.numpy as jnp
from jax import lax
from jax.experimental import pallas as pl
from jax.experimental.pallas import tpu as pltpu
from jax.sharding import PartitionSpec as P

GELU_COEF = 0.7978845608028654
MESH = pl.DeviceIdType.MESH
F32 = jnp.float32
BF16 = jnp.bfloat16
EDGE = 16
DIRS = [(a, b) for a in (-1, 0, 1) for b in (-1, 0, 1) if (a, b) != (0, 0)]
TAPS = 49
SMALL_TILES = 8


def gelu_pair(v):
    sq = v * v
    t = jnp.tanh(GELU_COEF * v * (1.0 + 0.044715 * sq))
    half = 0.5 * (1.0 + t)
    derivative = half + (0.5 * GELU_COEF) * v * (1.0 - t * t) * (1.0 + (3.0 * 0.044715) * sq)
    return v * half, derivative


def fold(x):
    return jnp.sum(x.reshape(x.shape[0] // 8, 8, x.shape[1]), axis=0)


def kernel(
    n_lat, n_lon, scale,
    mask, fields_hbm, *rest,
):
    sources, rest = (fields_hbm,) + rest[:10], rest[10:]
    block_out, grad_fields, grad_mlp, grad_kernel, grad_channels, grad_bias = rest[:6]
    cot, dk, dbias, gain, nbias, w_in, b_in, w_out, b_out, lscale = rest[6:16]
    (
    load_sem, pad, gpad, wide, xs, kb, dgrad, normed_s, gpre_s, hid_s, gout_s,
    packed, pair_recv, merged, mlp_recv, chan_acc, bias_acc, small, small_recv, small_sum, small_all,
    h_send, h_recv, g_send, g_recv, p_send, p_recv, m_send, m_recv, s_send, s_recv, a_send, a_recv, sync,
    ) = rest[16:]
    rows, cols, ch = cot.shape
    hid = w_in.shape[1]
    n_dev = n_lat * n_lon
    lat, lon = lax.axis_index("lat"), lax.axis_index("lon")
    me = lat * n_lon + lon
    per_lat = max(1, SMALL_TILES // n_lat)
    first_lon, lon_step = n_lon // 4, n_lon // (2 * per_lat)

    def where(flat):
        return {"lat": flat // n_lon, "lon": flat % n_lon}

    def peer(k):
        return (me + 1 + k) % n_dev

    barrier = pltpu.get_barrier_semaphore()

    def at(dlat, dlon):
        return {"lat": lat + dlat, "lon": (lon + dlon + n_lon) % n_lon}

    for dlat, dlon in DIRS:
        def greet():
            pl.semaphore_signal(barrier, inc=1, device_id=at(dlat, dlon), device_id_type=MESH)

        if dlat:
            pl.when((lat + dlat >= 0) & (lat + dlat < n_lat))(greet)
        else:
            greet()
    rows_beside = jnp.where(lat > 0, 1, 0) + jnp.where(lat < n_lat - 1, 1, 0)

    plane_size = 4 * n_lat - 1
    line_size = n_lon // 4 - 1

    def plane_signal(sem):
        @pl.loop(1, plane_size + 1)
        def _(k):
            place = (lat * 4 + lon % 4 + k) % (plane_size + 1)
            to = {"lat": place // 4, "lon": lon - lon % 4 + place % 4}
            pl.semaphore_signal(sem, inc=1, device_id=to, device_id_type=MESH)

    for k in range(1, line_size + 1):
        pl.semaphore_signal(barrier, inc=1, device_id=at(0, 4 * k), device_id_type=MESH)
    plane_signal(barrier)

    def halo(buf, send, recv, step, which=(-1, 0, 1)):
        cuts = {
            1: ((rows, rows + 3), (0, 3)),
            -1: ((3, 6), (rows + 3, rows + 6)),
            0: ((3, rows + 3), (3, rows + 3)),
        }
        cells = {
            1: ((cols, cols + EDGE), (0, EDGE)),
            -1: ((EDGE, 2 * EDGE), (cols + EDGE, cols + 2 * EDGE)),
            0: ((EDGE, cols + EDGE), (EDGE, cols + EDGE)),
        }
        for d, (dlat, dlon) in enumerate(DIRS):
            if dlat not in which:
                continue
            (s0, s1), (t0, t1) = cuts[dlat]
            (u0, u1), (v0, v1) = cells[dlon]
            copy = pltpu.make_async_remote_copy(
                src_ref=buf.at[pl.ds(s0, s1 - s0), pl.ds(u0, u1 - u0)],
                dst_ref=buf.at[pl.ds(t0, t1 - t0), pl.ds(v0, v1 - v0)],
                send_sem=send.at[d],
                recv_sem=recv.at[d],
                device_id={
                    "lat": lat + dlat,
                    "lon": (lon + dlon + n_lon) % n_lon,
                },
                device_id_type=MESH,
            )
            to = (lat + dlat >= 0) & (lat + dlat < n_lat)
            back = (lat - dlat >= 0) & (lat - dlat < n_lat)
            if step == "start":
                act, cond = copy.start, to
            elif step == "recv":
                act, cond = copy.wait_recv, back
            else:
                act, cond = copy.wait_send, to
            if dlat == 0:
                act()
            else:
                pl.when(cond)(act)

    center = pad.at[pl.ds(3, rows), pl.ds(EDGE, cols)]
    loads = [
        pltpu.make_async_copy(src, dst, load_sem.at[i])
        for i, (src, dst) in enumerate(zip(sources, (center,) + rest[6:16]))
    ]
    for load in loads:
        load.start()

    @pl.when(lat == 0)
    def _():
        pad[0:3] = jnp.zeros((3,) + pad.shape[1:], BF16)
        gpad[0:3] = jnp.zeros((3,) + pad.shape[1:], BF16)

    @pl.when(lat == n_lat - 1)
    def _():
        pad[rows + 3 : rows + 6] = jnp.zeros((3,) + pad.shape[1:], BF16)
        gpad[rows + 3 : rows + 6] = jnp.zeros((3,) + pad.shape[1:], BF16)

    chan_acc[...] = jnp.zeros(chan_acc.shape, F32)
    bias_acc[...] = jnp.zeros(bias_acc.shape, F32)
    small[SMALL_TILES - 1] = jnp.zeros((8, ch), F32)

    loads[0].wait()
    pl.semaphore_wait(barrier, 2 + 3 * rows_beside + line_size + plane_size)
    halo(pad, h_send, h_recv, "start")
    plane_signal(sync)
    for load in loads[1:]:
        load.wait()
    for a in range(7):
        for b in range(7):
            kb[a * 7 + b] = jnp.broadcast_to(dk[a, b : b + 1, :], (8, ch))

    def shifted(buf, start, stop):
        @pl.loop(start, stop)
        def _(r):
            wide[...] = buf[r].astype(F32)
            for b in range(7):
                xs[b, r] = wide[EDGE - 3 + b : EDGE - 3 + b + cols, :]

    def chunk(j):
        return pl.ds(pl.multiple_of(j * 8, 8), 8)

    def stencil(j, flip, inputs, acc):
        acc = list(acc)
        for b in range(7):
            taps = [kb[TAPS - 1 - (a * 7 + b) if flip else a * 7 + b] for a in range(7)]
            for r in inputs:
                x = xs[b, r, chunk(j), :]
                for i in range(max(0, r - 6), min(rows, r + 1)):
                    term = taps[r - i] * x
                    acc[i] = term if acc[i] is None else acc[i] + term
        return acc

    inner = range(3, rows + 3)
    outer = [r for r in range(rows + 6) if r not in inner]

    halo(pad, h_send, h_recv, "recv", (0,))
    shifted(pad, 3, rows + 3)

    @pl.loop(0, cols // 8)
    def _(j):
        for i, value in enumerate(stencil(j, False, inner, [None] * rows)):
            dgrad[i, chunk(j), :] = value + dbias[...]

    halo(pad, h_send, h_recv, "recv", (-1, 1))
    shifted(pad, 0, 3)
    shifted(pad, rows + 3, rows + 6)

    @pl.loop(0, cols // 8)
    def _(j):
        start = [dgrad[i, chunk(j), :] for i in range(rows)]
        for i, value in enumerate(stencil(j, False, outer, start)):
            dgrad[i, chunk(j), :] = value

    ocean = mask[0, 0].astype(F32)

    @pl.loop(0, rows // 2)
    def _(t):
        two = pl.ds(t * 2, 2)
        span = pl.ds(pl.multiple_of(t * 2 * cols, 2 * cols), 2 * cols)
        depth = dgrad[two].reshape(2 * cols, ch)
        cot_rows = cot[two].astype(F32).reshape(2 * cols, ch)
        centered = depth - jnp.sum(depth, axis=-1, keepdims=True) * (1.0 / ch)
        variance = jnp.sum(centered * centered, axis=-1, keepdims=True) * (1.0 / ch)
        inverse = lax.rsqrt(variance + 1e-06)
        normed = centered * inverse
        normed_low = (normed * gain[...] + nbias[...]).astype(BF16)
        pre = jnp.dot(normed_low, w_in[...], preferred_element_type=F32) + b_in[...]
        activated, derivative = gelu_pair(pre)
        hidden_low = activated.astype(BF16)
        out = jnp.dot(hidden_low, w_out[...], preferred_element_type=F32) + b_out[...]
        scaled = ocean * lscale[...]
        low = pad[pl.ds(3 + t * 2, 2), EDGE : cols + EDGE, :].astype(F32).reshape(2 * cols, ch) + scaled * out
        block_out[two] = low.astype(BF16).reshape(2, cols, ch)
        grad_out = scaled * cot_rows
        grad_out_low = grad_out.astype(BF16)
        nt = (((1,), (1,)), ((), ()))
        grad_hidden = lax.dot_general(grad_out_low, w_out[...], nt, preferred_element_type=F32)
        grad_pre = grad_hidden * derivative
        grad_pre_low = grad_pre.astype(BF16)
        grad_normed = lax.dot_general(grad_pre_low, w_in[...], nt, preferred_element_type=F32)
        grad_hat = grad_normed * gain[...]
        mean_hat = jnp.sum(grad_hat, axis=-1, keepdims=True) * (1.0 / ch)
        mean_dot = jnp.sum(grad_hat * normed, axis=-1, keepdims=True) * (1.0 / ch)
        grad_depth = inverse * (grad_hat - mean_hat - normed * mean_dot)
        dgrad[two] = grad_depth.reshape(2, cols, ch)
        gpad[pl.ds(3 + t * 2, 2), EDGE : cols + EDGE, :] = grad_depth.astype(BF16).reshape(2, cols, ch)
        normed_s[span, :] = normed_low
        gpre_s[span, :] = grad_pre_low
        hid_s[span, :] = hidden_low
        gout_s[span, :] = grad_out_low
        chan_acc[0] += fold(grad_depth)
        chan_acc[1] += fold(grad_normed * normed)
        chan_acc[2] += fold(grad_normed)
        chan_acc[3] += fold(grad_out)
        chan_acc[4] += fold(ocean * out * cot_rows)
        bias_acc[...] += fold(grad_pre)

    halo(gpad, g_send, g_recv, "start")
    pl.semaphore_wait(sync, plane_size)

    part = ch // n_lat
    units, half = hid // n_lon, n_lon // 2
    parity = lon % 2
    tt = (((0,), (0,)), ((), ()))
    win_t = lax.dot_general(normed_s[...], gpre_s[...], tt, preferred_element_type=F32).T
    wout_t = lax.dot_general(gout_s[...], hid_s[...], tt, preferred_element_type=F32).T
    lane = lax.broadcasted_iota(jnp.int32, (hid, ch), 1)
    for t in range(n_lat):
        first = pltpu.roll(win_t, (ch - part * t) % ch, 1) if t else win_t
        shift = (part - part * t) % ch
        second = pltpu.roll(wout_t, shift, 1) if shift else wout_t
        both = jnp.where(lane < part, first, second).astype(BF16)
        both = both.reshape(half, 2, units, ch)
        for q in range(2):
            packed[q, t] = both[:, q]

    pair = pltpu.make_async_remote_copy(
        src_ref=packed.at[1 - parity],
        dst_ref=pair_recv,
        send_sem=p_send,
        recv_sem=p_recv,
        device_id={"lat": lat, "lon": lon + 1 - 2 * parity},
        device_id_type=MESH,
    )
    pair.start()

    for b in range(7):

        def add_chunk(j, sums):
            x = xs[b, :, chunk(j), :]
            g = dgrad[:, chunk(j), :]
            return tuple(sums[a] + jnp.sum(x[a : a + rows] * g, axis=0) for a in range(7))

        zero = jnp.zeros((8, ch), F32)
        sums = lax.fori_loop(0, cols // 8, add_chunk, (zero,) * 7)
        for a in range(7):
            row = a * 7 + b
            small[row // 8, row % 8 : row % 8 + 1, :] = jnp.sum(sums[a], axis=0, keepdims=True)
    for i in range(5):
        row = TAPS + i
        small[row // 8, row % 8 : row % 8 + 1, :] = jnp.sum(chan_acc[i], axis=0, keepdims=True)
    bias_row = jnp.sum(bias_acc[...], axis=0, keepdims=True)
    for i in range(hid // ch):
        row = TAPS + 5 + i
        small[row // 8, row % 8 : row % 8 + 1, :] = bias_row[:, i * ch : (i + 1) * ch]

    def owner_of(t):
        return t // per_lat * n_lon + first_lon + t % per_lat * lon_step

    def small_copy(t):
        owner = owner_of(t)
        return pltpu.make_async_remote_copy(
            src_ref=small.at[t],
            dst_ref=small_recv.at[(owner - me - 1 + n_dev) % n_dev],
            send_sem=s_send.at[t],
            recv_sem=s_recv,
            device_id=where(owner),
            device_id_type=MESH,
        )

    for t in range(SMALL_TILES):

        @pl.when(me != owner_of(t))
        def _():
            small_copy(t).start()

    group = n_lat * half
    mine = lat * half + lon // 2

    def mlp_copy(k):
        to = (mine + 1 + k) % group
        return pltpu.make_async_remote_copy(
            src_ref=merged.at[to // half, to % half],
            dst_ref=mlp_recv.at[k],
            send_sem=m_send,
            recv_sem=m_recv,
            device_id={"lat": to // half, "lon": 2 * (to % half) + parity},
            device_id_type=MESH,
        )

    pair.wait_recv()
    merged[...] = (packed[parity].astype(F32) + pair_recv[...].astype(F32)).astype(BF16)

    @pl.loop(0, group - 1)
    def _(k):
        mlp_copy(k).start()

    halo(gpad, g_send, g_recv, "recv")
    shifted(gpad, 0, rows + 6)

    tile = lat * per_lat + (lon - first_lon) // lon_step
    is_owner = (lat < SMALL_TILES // per_lat) & (lon >= first_lon) & (lon < first_lon + per_lat * lon_step)
    is_owner = is_owner & ((lon - first_lon) % lon_step == 0)

    def gather_copy(k):
        return pltpu.make_async_remote_copy(
            src_ref=small_sum,
            dst_ref=small_all.at[tile],
            send_sem=a_send,
            recv_sem=a_recv.at[tile],
            device_id=where(peer(k)),
            device_id_type=MESH,
        )

    @pl.when(is_owner)
    def _():
        pltpu.make_async_copy(small_recv, small_recv, s_recv).wait()
        total = lax.fori_loop(0, n_dev - 1, lambda k, acc: acc + small_recv[k], small[tile])
        small_sum[...] = total * scale
        small_all[tile] = total * scale

        @pl.loop(0, n_dev - 1)
        def _(k):
            gather_copy(k).start()

    @pl.loop(0, cols // 16)
    def _(j):
        two = [stencil(2 * j + h, True, range(rows + 6), [None] * rows) for h in range(2)]
        cells = pl.ds(pl.multiple_of(j * 16, 16), 16)
        for i in range(rows):
            value = jnp.concatenate([two[0][i], two[1][i]], axis=0)
            grad_fields[i, cells, :] = (cot[i, cells, :].astype(F32) + value).astype(BF16)

    pltpu.make_async_copy(mlp_recv, mlp_recv, m_recv).wait()
    own = merged[lat, lon // 2].astype(F32)
    total = lax.fori_loop(0, group - 1, lambda k, acc: acc + mlp_recv[k].astype(F32), own)
    total = total * scale
    grad_mlp[0] = total[:, 0:part]
    grad_mlp[1] = total[:, part : 2 * part]

    for t in range(SMALL_TILES):

        @pl.when(me != owner_of(t))
        def _():
            pltpu.make_async_copy(small_sum, small_all.at[t], a_recv.at[t]).wait()

    for a in range(7):
        for b in range(7):
            row = a * 7 + b
            grad_kernel[a, b : b + 1, :] = small_all[row // 8, row % 8 : row % 8 + 1, :]
    for i in range(5):
        row = TAPS + i
        grad_channels[i : i + 1, :] = small_all[row // 8, row % 8 : row % 8 + 1, :]
    for i in range(hid // ch):
        row = TAPS + 5 + i
        grad_bias[:, i * ch : (i + 1) * ch] = small_all[row // 8, row % 8 : row % 8 + 1, :]

    halo(pad, h_send, h_recv, "sent")
    halo(gpad, g_send, g_recv, "sent")
    pair.wait_send()
    pltpu.make_async_copy(mlp_recv, mlp_recv, m_send).wait()
    for t in range(SMALL_TILES):

        @pl.when(me != owner_of(t))
        def _():
            small_copy(t).wait_send()

    @pl.when(is_owner)
    def _():
        pltpu.make_async_copy(small_recv, small_recv, a_send).wait()


def store_kernel(*refs):
    n = len(refs) // 2
    copies = [pltpu.make_async_copy(refs[i], refs[n + i], refs[-1].at[i]) for i in range(n)]
    for copy in copies:
        copy.start()
    for copy in copies:
        copy.wait()


def store(arrays):
    return pl.pallas_call(
        store_kernel,
        out_shape=[pltpu.HBM(x.shape, x.dtype) for x in arrays],
        in_specs=[pl.BlockSpec(memory_space=pltpu.VMEM)] * len(arrays),
        out_specs=[pl.BlockSpec(memory_space=pltpu.HBM)] * len(arrays),
        scratch_shapes=[pltpu.SemaphoreType.DMA((len(arrays),))],
    )(*[pltpu.with_memory_space_constraint(x, pltpu.VMEM) for x in arrays])


def body(mesh_shape, fields, cotangent, ocean_mask, depth_kernel, depth_bias, norm_gain, norm_bias,
         weight_in, bias_in, weight_out, bias_out, layer_scale):
    n_lat, n_lon = mesh_shape
    n_dev = n_lat * n_lon
    rows, cols, ch = fields.shape
    hid = weight_in.shape[1]
    units, part, cells = hid // n_lon, ch // n_lat, rows * cols
    scale = 1.0 / math.sqrt(cells * n_dev)
    vmem = pl.BlockSpec(memory_space=pltpu.VMEM)
    shares = (n_lat, n_lon // 2, units, ch)
    padded = (rows + 6, cols + 2 * EDGE, ch)
    operands = (
        fields, cotangent, depth_kernel, depth_bias.reshape(1, ch), norm_gain.reshape(1, ch),
        norm_bias.reshape(1, ch), weight_in, bias_in.reshape(1, hid), weight_out,
        bias_out.reshape(1, ch), layer_scale.reshape(1, ch),
    )
    outs = pl.pallas_call(
        functools.partial(kernel, n_lat, n_lon, scale),
        out_shape=[
            jax.ShapeDtypeStruct(fields.shape, BF16),
            jax.ShapeDtypeStruct(fields.shape, BF16),
            jax.ShapeDtypeStruct((2, units, part), F32),
            jax.ShapeDtypeStruct((7, 7, ch), F32),
            jax.ShapeDtypeStruct((5, ch), F32),
            jax.ShapeDtypeStruct((1, hid), F32),
        ],
        in_specs=[pl.BlockSpec(memory_space=pltpu.SMEM)] + [pl.BlockSpec(memory_space=pltpu.HBM)] * 11,
        out_specs=[vmem] * 6,
        scratch_shapes=[pltpu.VMEM(x.shape, x.dtype) for x in operands[1:]]
        + [
            pltpu.SemaphoreType.DMA((11,)),
            pltpu.VMEM(padded, BF16),
            pltpu.VMEM(padded, BF16),
            pltpu.VMEM(padded[1:], F32),
            pltpu.VMEM((7, rows + 6, cols, ch), F32),
            pltpu.VMEM((TAPS, 8, ch), F32),
            pltpu.VMEM((rows, cols, ch), F32),
            pltpu.VMEM((cells, ch), BF16),
            pltpu.VMEM((cells, hid), BF16),
            pltpu.VMEM((cells, hid), BF16),
            pltpu.VMEM((cells, ch), BF16),
            pltpu.VMEM((2,) + shares, BF16),
            pltpu.VMEM(shares, BF16),
            pltpu.VMEM(shares, BF16),
            pltpu.VMEM((n_dev // 2 - 1, units, ch), BF16),
            pltpu.VMEM((5, 8, ch), F32),
            pltpu.VMEM((8, hid), F32),
            pltpu.VMEM((SMALL_TILES, 8, ch), F32),
            pltpu.VMEM((n_dev - 1, 8, ch), F32),
            pltpu.VMEM((8, ch), F32),
            pltpu.VMEM((SMALL_TILES, 8, ch), F32),
            pltpu.SemaphoreType.DMA((8,)),
            pltpu.SemaphoreType.DMA((8,)),
            pltpu.SemaphoreType.DMA((8,)),
            pltpu.SemaphoreType.DMA((8,)),
            pltpu.SemaphoreType.DMA,
            pltpu.SemaphoreType.DMA,
            pltpu.SemaphoreType.DMA,
            pltpu.SemaphoreType.DMA,
            pltpu.SemaphoreType.DMA((SMALL_TILES,)),
            pltpu.SemaphoreType.DMA,
            pltpu.SemaphoreType.DMA,
            pltpu.SemaphoreType.DMA((SMALL_TILES,)),
            pltpu.SemaphoreType.REGULAR,
        ],
        compiler_params=pltpu.CompilerParams(
            collective_id=0, has_side_effects=True, vmem_limit_bytes=48 << 20
        ),
    )(ocean_mask, *[pltpu.with_memory_space_constraint(x, pltpu.HBM) for x in operands])
    outs = store(outs)
    return (outs[0], outs[1], outs[2].transpose(0, 2, 1), outs[3], outs[4], outs[5].reshape(hid))


def solution(mesh):
    tiled = P("lat", "lon", None)
    placed = (tiled, tiled, P("lat", "lon")) + (P(),) * 9
    return jax.shard_map(
        functools.partial(body, (mesh.shape["lat"], mesh.shape["lon"])),
        mesh=mesh,
        in_specs=placed,
        out_specs=(tiled, tiled, P(None, "lat", "lon"), P(), P(), P()),
        check_vma=False,
    )
```

```python
import functools
import math

import jax
import jax.numpy as jnp
from jax import lax
from jax.experimental import pallas as pl
from jax.experimental.pallas import tpu as pltpu
from jax.sharding import PartitionSpec as P

GELU_COEF = 0.7978845608028654
MESH = pl.DeviceIdType.MESH
F32 = jnp.float32
BF16 = jnp.bfloat16
EDGE = 16
DIRS = [(a, b) for a in (-1, 0, 1) for b in (-1, 0, 1) if (a, b) != (0, 0)]
TAPS = 49
SMALL_TILES = 8


def gelu_pair(v):
    sq = v * v
    t = jnp.tanh(GELU_COEF * v * (1.0 + 0.044715 * sq))
    half = 0.5 * (1.0 + t)
    derivative = half + (0.5 * GELU_COEF) * v * (1.0 - t * t) * (1.0 + (3.0 * 0.044715) * sq)
    return v * half, derivative


def fold(x):
    return jnp.sum(x.reshape(x.shape[0] // 8, 8, x.shape[1]), axis=0)


def kernel(
    n_lat, n_lon, scale,
    mask, fields_hbm, *rest,
):
    sources, rest = (fields_hbm,) + rest[:10], rest[10:]
    block_out, grad_fields, grad_mlp, grad_kernel, grad_channels, grad_bias = rest[:6]
    cot, dk, dbias, gain, nbias, w_in, b_in, w_out, b_out, lscale = rest[6:16]
    (
    load_sem, pad, gpad, wide, xs, kb, ksum, dgrad, normed_s, gpre_s, hid_s, gout_s,
    packed, pair_recv, merged, mlp_recv, chan_acc, bias_acc, small, small_recv, small_sum, small_all,
    h_send, h_recv, g_send, g_recv, p_send, p_recv, m_send, m_recv, s_send, s_recv, a_send, a_recv, sync,
    ) = rest[16:]
    rows, cols, ch = cot.shape
    hid = w_in.shape[1]
    n_dev = n_lat * n_lon
    lat, lon = lax.axis_index("lat"), lax.axis_index("lon")
    me = lat * n_lon + lon
    per_lat = max(1, SMALL_TILES // n_lat)
    first_lon, lon_step = n_lon // 4, n_lon // (2 * per_lat)

    def where(flat):
        return {"lat": flat // n_lon, "lon": flat % n_lon}

    def peer(k):
        return (me + 1 + k) % n_dev

    barrier = pltpu.get_barrier_semaphore()

    def at(dlat, dlon):
        return {"lat": lat + dlat, "lon": (lon + dlon + n_lon) % n_lon}

    for dlat, dlon in DIRS:
        def greet():
            pl.semaphore_signal(barrier, inc=1, device_id=at(dlat, dlon), device_id_type=MESH)

        if dlat:
            pl.when((lat + dlat >= 0) & (lat + dlat < n_lat))(greet)
        else:
            greet()
    rows_beside = jnp.where(lat > 0, 1, 0) + jnp.where(lat < n_lat - 1, 1, 0)

    plane_size = 4 * n_lat - 1
    line_size = n_lon // 4 - 1

    def plane_signal(sem):
        @pl.loop(1, plane_size + 1)
        def _(k):
            place = (lat * 4 + lon % 4 + k) % (plane_size + 1)
            to = {"lat": place // 4, "lon": lon - lon % 4 + place % 4}
            pl.semaphore_signal(sem, inc=1, device_id=to, device_id_type=MESH)

    for k in range(1, line_size + 1):
        pl.semaphore_signal(barrier, inc=1, device_id=at(0, 4 * k), device_id_type=MESH)
    plane_signal(barrier)

    def halo(buf, send, recv, step, which=(-1, 0, 1)):
        cuts = {
            1: ((rows, rows + 3), (0, 3)),
            -1: ((3, 6), (rows + 3, rows + 6)),
            0: ((3, rows + 3), (3, rows + 3)),
        }
        cells = {
            1: ((cols, cols + EDGE), (0, EDGE)),
            -1: ((EDGE, 2 * EDGE), (cols + EDGE, cols + 2 * EDGE)),
            0: ((EDGE, cols + EDGE), (EDGE, cols + EDGE)),
        }
        for d, (dlat, dlon) in enumerate(DIRS):
            if dlat not in which:
                continue
            (s0, s1), (t0, t1) = cuts[dlat]
            (u0, u1), (v0, v1) = cells[dlon]
            copy = pltpu.make_async_remote_copy(
                src_ref=buf.at[pl.ds(s0, s1 - s0), pl.ds(u0, u1 - u0)],
                dst_ref=buf.at[pl.ds(t0, t1 - t0), pl.ds(v0, v1 - v0)],
                send_sem=send.at[d],
                recv_sem=recv.at[d],
                device_id={
                    "lat": lat + dlat,
                    "lon": (lon + dlon + n_lon) % n_lon,
                },
                device_id_type=MESH,
            )
            to = (lat + dlat >= 0) & (lat + dlat < n_lat)
            back = (lat - dlat >= 0) & (lat - dlat < n_lat)
            if step == "start":
                act, cond = copy.start, to
            elif step == "recv":
                act, cond = copy.wait_recv, back
            else:
                act, cond = copy.wait_send, to
            if dlat == 0:
                act()
            else:
                pl.when(cond)(act)

    center = pad.at[pl.ds(3, rows), pl.ds(EDGE, cols)]
    loads = [
        pltpu.make_async_copy(src, dst, load_sem.at[i])
        for i, (src, dst) in enumerate(zip(sources, (center,) + rest[6:16]))
    ]
    for load in loads:
        load.start()

    @pl.when(lat == 0)
    def _():
        pad[0:3] = jnp.zeros((3,) + pad.shape[1:], BF16)
        gpad[0:3] = jnp.zeros((3,) + pad.shape[1:], BF16)

    @pl.when(lat == n_lat - 1)
    def _():
        pad[rows + 3 : rows + 6] = jnp.zeros((3,) + pad.shape[1:], BF16)
        gpad[rows + 3 : rows + 6] = jnp.zeros((3,) + pad.shape[1:], BF16)

    chan_acc[...] = jnp.zeros(chan_acc.shape, F32)
    bias_acc[...] = jnp.zeros(bias_acc.shape, F32)
    small[SMALL_TILES - 1] = jnp.zeros((8, ch), F32)

    loads[0].wait()
    pl.semaphore_wait(barrier, 2 + 3 * rows_beside + line_size + plane_size)
    halo(pad, h_send, h_recv, "start")
    plane_signal(sync)
    for load in loads[1:]:
        load.wait()
    for a in range(7):
        for b in range(7):
            kb[a * 7 + b] = jnp.broadcast_to(dk[a, b : b + 1, :], (8, ch))

    def shifted(buf, start, stop):
        @pl.loop(start, stop)
        def _(r):
            wide[...] = buf[r].astype(F32)
            for b in range(7):
                xs[b, r] = wide[EDGE - 3 + b : EDGE - 3 + b + cols, :]

    def chunk(j):
        return pl.ds(pl.multiple_of(j * 8, 8), 8)

    def stencil(j, flip, inputs, acc):
        acc = list(acc)
        for b in range(7):
            taps = [kb[TAPS - 1 - (a * 7 + b) if flip else a * 7 + b] for a in range(7)]
            for r in inputs:
                x = xs[b, r, chunk(j), :]
                for i in range(max(0, r - 6), min(rows, r + 1)):
                    term = taps[r - i] * x
                    acc[i] = term if acc[i] is None else acc[i] + term
        return acc

    inner = range(3, rows + 3)
    chunks = cols // 8
    some = rows // 2
    near = jnp.where(lat == 0, 0, some)
    far = some - near
    ocean = mask[0, 0].astype(F32)

    @pl.loop(3, rows + 3)
    def _(r):
        wide[EDGE : EDGE + cols, :] = pad[r, EDGE : EDGE + cols, :].astype(F32)
        for b in range(7):
            xs[b, r, 8 : cols - 8, :] = wide[EDGE + 5 + b : EDGE + 5 + b + cols - 16, :]

    @pl.loop(1, chunks - 1)
    def _(j):
        for i, value in enumerate(stencil(j, False, inner, [None] * rows)):
            dgrad[i, chunk(j), :] = value + dbias[...]

    def finish():
        halo(pad, h_send, h_recv, "recv")

        @pl.loop(3, rows + 3)
        def _(r):
            wide[0 : 2 * EDGE, :] = pad[r, 0 : 2 * EDGE, :].astype(F32)
            wide[cols : cols + 2 * EDGE, :] = pad[r, cols : cols + 2 * EDGE, :].astype(F32)
            for b in range(7):
                xs[b, r, 0:8, :] = wide[EDGE - 3 + b : EDGE + 5 + b, :]
                xs[b, r, cols - 8 : cols, :] = wide[cols + EDGE - 11 + b : cols + EDGE - 3 + b, :]

        shifted(pad, 0, 3)
        shifted(pad, rows + 3, rows + 6)

        @pl.loop(0, 2)
        def _(k):
            j = k * (chunks - 1)
            for i, value in enumerate(stencil(j, False, range(rows + 6), [None] * rows)):
                dgrad[i, chunk(j), :] = value + dbias[...]

        def side(inputs):
            taken = [i for i in range(rows) if any(0 <= r - i < 7 for r in inputs)]

            @pl.loop(0, chunks // 2 - 1)
            def _(k):
                for j in (2 * k + 1, 2 * k + 2):
                    start = [dgrad[i, chunk(j), :] if i in taken else None for i in range(rows)]
                    values = stencil(j, False, inputs, start)
                    for i in taken:
                        dgrad[i, chunk(j), :] = values[i]

        pl.when(lat > 0)(functools.partial(side, range(3)))
        pl.when(lat < n_lat - 1)(functools.partial(side, range(rows + 3, rows + 6)))

    def mlp(read, write, start, count):
        span = pl.ds(start, count)
        depth = read(dgrad, 0, 0)
        cot_rows = read(cot, 0, 0).astype(F32)
        centered = depth - jnp.sum(depth, axis=-1, keepdims=True) * (1.0 / ch)
        variance = jnp.sum(centered * centered, axis=-1, keepdims=True) * (1.0 / ch)
        inverse = lax.rsqrt(variance + 1e-06)
        normed = centered * inverse
        normed_low = (normed * gain[...] + nbias[...]).astype(BF16)
        pre = jnp.dot(normed_low, w_in[...], preferred_element_type=F32) + b_in[...]
        activated, derivative = gelu_pair(pre)
        hidden_low = activated.astype(BF16)
        out = jnp.dot(hidden_low, w_out[...], preferred_element_type=F32) + b_out[...]
        scaled = ocean * lscale[...]
        write(block_out, 0, 0, (read(pad, 3, EDGE).astype(F32) + scaled * out).astype(BF16))
        grad_out = scaled * cot_rows
        grad_out_low = grad_out.astype(BF16)
        nt = (((1,), (1,)), ((), ()))
        grad_hidden = lax.dot_general(grad_out_low, w_out[...], nt, preferred_element_type=F32)
        grad_pre = grad_hidden * derivative
        grad_pre_low = grad_pre.astype(BF16)
        grad_normed = lax.dot_general(grad_pre_low, w_in[...], nt, preferred_element_type=F32)
        grad_hat = grad_normed * gain[...]
        mean_hat = jnp.sum(grad_hat, axis=-1, keepdims=True) * (1.0 / ch)
        mean_dot = jnp.sum(grad_hat * normed, axis=-1, keepdims=True) * (1.0 / ch)
        grad_depth = inverse * (grad_hat - mean_hat - normed * mean_dot)
        write(dgrad, 0, 0, grad_depth)
        write(gpad, 3, EDGE, grad_depth.astype(BF16))
        normed_s[span, :] = normed_low
        gpre_s[span, :] = grad_pre_low
        hid_s[span, :] = hidden_low
        gout_s[span, :] = grad_out_low
        chan_acc[0] += fold(grad_depth)
        chan_acc[1] += fold(grad_normed * normed)
        chan_acc[2] += fold(grad_normed)
        chan_acc[3] += fold(grad_out)
        chan_acc[4] += fold(ocean * out * cot_rows)
        bias_acc[...] += fold(grad_pre)

    def strip(first, count, lo, hi):
        size = count * (hi - lo)

        def read(buf, above, before):
            return buf[pl.ds(above + first, count), before + lo : before + hi, :].reshape(size, ch)

        def write(buf, above, before, value):
            buf[pl.ds(above + first, count), before + lo : before + hi, :] = value.reshape(count, hi - lo, ch)

        return read, write

    def read_ends(buf, above, before):
        band = pl.ds(above + near, some)
        ends = [buf[band, before + c : before + c + 16, :] for c in (0, cols - 16)]
        return jnp.concatenate([end.reshape(some * 16, ch) for end in ends], axis=0)

    def write_ends(buf, above, before, value):
        band = pl.ds(above + near, some)
        for k, c in enumerate((0, cols - 16)):
            end = value[k * some * 16 : (k + 1) * some * 16]
            buf[band, before + c : before + c + 16, :] = end.reshape(some, 16, ch)

    def kernel_sums(b, first, js, sums):
        sums = list(sums)
        for j in js:
            x = xs[b, pl.ds(first, some + 6), chunk(j), :]
            g = dgrad[pl.ds(first, some), chunk(j), :]
            for a in range(7):
                sums[a] = sums[a] + jnp.sum(x[a : a + some] * g, axis=0)
        return tuple(sums)

    core = some * (cols - 32)
    ends = some * 32
    if n_lat > 2:
        pl.when((lat > 0) & (lat < n_lat - 1))(finish)

    @pl.loop(0, some // 2)
    def _(t):
        mlp(*strip(near + 2 * t, 2, 16, cols - 16), pl.multiple_of(t * (core * 2 // some), 16), core * 2 // some)

    zero = jnp.zeros((8, ch), F32)
    for b in range(7):
        sums = lax.fori_loop(
            1, chunks // 2 - 1, lambda k, sums: kernel_sums(b, near, (2 * k, 2 * k + 1), sums), (zero,) * 7
        )
        for a in range(7):
            ksum[a * 7 + b] = sums[a]

    if n_lat > 2:
        pl.when((lat == 0) | (lat == n_lat - 1))(finish)
    else:
        finish()

    mlp(read_ends, write_ends, core, ends)

    @pl.loop(0, some // 2)
    def _(t):
        mlp(*strip(far + 2 * t, 2, 0, cols), pl.multiple_of(core + ends + t * 2 * cols, 16), 2 * cols)

    halo(gpad, g_send, g_recv, "start")
    pl.semaphore_wait(sync, plane_size)

    for b in range(7):
        sums = tuple(ksum[a * 7 + b] for a in range(7))
        sums = kernel_sums(b, near, (0, 1, chunks - 2, chunks - 1), sums)
        sums = lax.fori_loop(
            0, chunks // 2, lambda k, sums: kernel_sums(b, far, (2 * k, 2 * k + 1), sums), sums
        )
        for a in range(7):
            row = a * 7 + b
            small[row // 8, row % 8 : row % 8 + 1, :] = jnp.sum(sums[a], axis=0, keepdims=True)
    for i in range(5):
        row = TAPS + i
        small[row // 8, row % 8 : row % 8 + 1, :] = jnp.sum(chan_acc[i], axis=0, keepdims=True)
    bias_row = jnp.sum(bias_acc[...], axis=0, keepdims=True)
    for i in range(hid // ch):
        row = TAPS + 5 + i
        small[row // 8, row % 8 : row % 8 + 1, :] = bias_row[:, i * ch : (i + 1) * ch]

    def owner_of(t):
        return t // per_lat * n_lon + first_lon + t % per_lat * lon_step

    def small_copy(t):
        owner = owner_of(t)
        return pltpu.make_async_remote_copy(
            src_ref=small.at[t],
            dst_ref=small_recv.at[(owner - me - 1 + n_dev) % n_dev],
            send_sem=s_send.at[t],
            recv_sem=s_recv,
            device_id=where(owner),
            device_id_type=MESH,
        )

    for t in range(SMALL_TILES):

        @pl.when(me != owner_of(t))
        def _():
            small_copy(t).start()

    part = ch // n_lat
    units, half = hid // n_lon, n_lon // 2
    parity = lon % 2
    tt = (((0,), (0,)), ((), ()))
    win_t = lax.dot_general(normed_s[...], gpre_s[...], tt, preferred_element_type=F32).T
    wout_t = lax.dot_general(gout_s[...], hid_s[...], tt, preferred_element_type=F32).T
    lane = lax.broadcasted_iota(jnp.int32, (hid, ch), 1)
    for t in range(n_lat):
        first = pltpu.roll(win_t, (ch - part * t) % ch, 1) if t else win_t
        shift = (part - part * t) % ch
        second = pltpu.roll(wout_t, shift, 1) if shift else wout_t
        both = jnp.where(lane < part, first, second).astype(BF16)
        both = both.reshape(half, 2, units, ch)
        for q in range(2):
            packed[q, t] = both[:, q]

    pair = pltpu.make_async_remote_copy(
        src_ref=packed.at[1 - parity],
        dst_ref=pair_recv,
        send_sem=p_send,
        recv_sem=p_recv,
        device_id={"lat": lat, "lon": lon + 1 - 2 * parity},
        device_id_type=MESH,
    )
    pair.start()

    group = n_lat * half
    mine = lat * half + lon // 2

    def mlp_copy(k):
        to = (mine + 1 + k) % group
        return pltpu.make_async_remote_copy(
            src_ref=merged.at[to // half, to % half],
            dst_ref=mlp_recv.at[k],
            send_sem=m_send,
            recv_sem=m_recv,
            device_id={"lat": to // half, "lon": 2 * (to % half) + parity},
            device_id_type=MESH,
        )

    pair.wait_recv()
    merged[...] = (packed[parity].astype(F32) + pair_recv[...].astype(F32)).astype(BF16)

    @pl.loop(0, group - 1)
    def _(k):
        mlp_copy(k).start()

    halo(gpad, g_send, g_recv, "recv")
    shifted(gpad, 0, rows + 6)

    tile = lat * per_lat + (lon - first_lon) // lon_step
    is_owner = (lat < SMALL_TILES // per_lat) & (lon >= first_lon) & (lon < first_lon + per_lat * lon_step)
    is_owner = is_owner & ((lon - first_lon) % lon_step == 0)

    def gather_copy(k):
        return pltpu.make_async_remote_copy(
            src_ref=small_sum,
            dst_ref=small_all.at[tile],
            send_sem=a_send,
            recv_sem=a_recv.at[tile],
            device_id=where(peer(k)),
            device_id_type=MESH,
        )

    @pl.when(is_owner)
    def _():
        pltpu.make_async_copy(small_recv, small_recv, s_recv).wait()
        total = lax.fori_loop(0, n_dev - 1, lambda k, acc: acc + small_recv[k], small[tile])
        small_sum[...] = total * scale
        small_all[tile] = total * scale

        @pl.loop(0, n_dev - 1)
        def _(k):
            gather_copy(k).start()

    @pl.loop(0, cols // 16)
    def _(j):
        two = [stencil(2 * j + h, True, range(rows + 6), [None] * rows) for h in range(2)]
        cells = pl.ds(pl.multiple_of(j * 16, 16), 16)
        for i in range(rows):
            value = jnp.concatenate([two[0][i], two[1][i]], axis=0)
            grad_fields[i, cells, :] = (cot[i, cells, :].astype(F32) + value).astype(BF16)

    pltpu.make_async_copy(mlp_recv, mlp_recv, m_recv).wait()
    own = merged[lat, lon // 2].astype(F32)
    total = lax.fori_loop(0, group - 1, lambda k, acc: acc + mlp_recv[k].astype(F32), own)
    total = total * scale
    grad_mlp[0] = total[:, 0:part]
    grad_mlp[1] = total[:, part : 2 * part]

    for t in range(SMALL_TILES):

        @pl.when(me != owner_of(t))
        def _():
            pltpu.make_async_copy(small_sum, small_all.at[t], a_recv.at[t]).wait()

    for a in range(7):
        for b in range(7):
            row = a * 7 + b
            grad_kernel[a, b : b + 1, :] = small_all[row // 8, row % 8 : row % 8 + 1, :]
    for i in range(5):
        row = TAPS + i
        grad_channels[i : i + 1, :] = small_all[row // 8, row % 8 : row % 8 + 1, :]
    for i in range(hid // ch):
        row = TAPS + 5 + i
        grad_bias[:, i * ch : (i + 1) * ch] = small_all[row // 8, row % 8 : row % 8 + 1, :]

    halo(pad, h_send, h_recv, "sent")
    halo(gpad, g_send, g_recv, "sent")
    pair.wait_send()
    pltpu.make_async_copy(mlp_recv, mlp_recv, m_send).wait()
    for t in range(SMALL_TILES):

        @pl.when(me != owner_of(t))
        def _():
            small_copy(t).wait_send()

    @pl.when(is_owner)
    def _():
        pltpu.make_async_copy(small_recv, small_recv, a_send).wait()


def store_kernel(*refs):
    n = len(refs) // 2
    copies = [pltpu.make_async_copy(refs[i], refs[n + i], refs[-1].at[i]) for i in range(n)]
    for copy in copies:
        copy.start()
    for copy in copies:
        copy.wait()


def store(arrays):
    return pl.pallas_call(
        store_kernel,
        out_shape=[pltpu.HBM(x.shape, x.dtype) for x in arrays],
        in_specs=[pl.BlockSpec(memory_space=pltpu.VMEM)] * len(arrays),
        out_specs=[pl.BlockSpec(memory_space=pltpu.HBM)] * len(arrays),
        scratch_shapes=[pltpu.SemaphoreType.DMA((len(arrays),))],
    )(*[pltpu.with_memory_space_constraint(x, pltpu.VMEM) for x in arrays])


def body(mesh_shape, fields, cotangent, ocean_mask, depth_kernel, depth_bias, norm_gain, norm_bias,
         weight_in, bias_in, weight_out, bias_out, layer_scale):
    n_lat, n_lon = mesh_shape
    n_dev = n_lat * n_lon
    rows, cols, ch = fields.shape
    hid = weight_in.shape[1]
    units, part, cells = hid // n_lon, ch // n_lat, rows * cols
    scale = 1.0 / math.sqrt(cells * n_dev)
    vmem = pl.BlockSpec(memory_space=pltpu.VMEM)
    shares = (n_lat, n_lon // 2, units, ch)
    padded = (rows + 6, cols + 2 * EDGE, ch)
    operands = (
        fields, cotangent, depth_kernel, depth_bias.reshape(1, ch), norm_gain.reshape(1, ch),
        norm_bias.reshape(1, ch), weight_in, bias_in.reshape(1, hid), weight_out,
        bias_out.reshape(1, ch), layer_scale.reshape(1, ch),
    )
    outs = pl.pallas_call(
        functools.partial(kernel, n_lat, n_lon, scale),
        out_shape=[
            jax.ShapeDtypeStruct(fields.shape, BF16),
            jax.ShapeDtypeStruct(fields.shape, BF16),
            jax.ShapeDtypeStruct((2, units, part), F32),
            jax.ShapeDtypeStruct((7, 7, ch), F32),
            jax.ShapeDtypeStruct((5, ch), F32),
            jax.ShapeDtypeStruct((1, hid), F32),
        ],
        in_specs=[pl.BlockSpec(memory_space=pltpu.SMEM)] + [pl.BlockSpec(memory_space=pltpu.HBM)] * 11,
        out_specs=[vmem] * 6,
        scratch_shapes=[pltpu.VMEM(x.shape, x.dtype) for x in operands[1:]]
        + [
            pltpu.SemaphoreType.DMA((11,)),
            pltpu.VMEM(padded, BF16),
            pltpu.VMEM(padded, BF16),
            pltpu.VMEM(padded[1:], F32),
            pltpu.VMEM((7, rows + 6, cols, ch), F32),
            pltpu.VMEM((TAPS, 8, ch), F32),
            pltpu.VMEM((TAPS, 8, ch), F32),
            pltpu.VMEM((rows, cols, ch), F32),
            pltpu.VMEM((cells, ch), BF16),
            pltpu.VMEM((cells, hid), BF16),
            pltpu.VMEM((cells, hid), BF16),
            pltpu.VMEM((cells, ch), BF16),
            pltpu.VMEM((2,) + shares, BF16),
            pltpu.VMEM(shares, BF16),
            pltpu.VMEM(shares, BF16),
            pltpu.VMEM((n_dev // 2 - 1, units, ch), BF16),
            pltpu.VMEM((5, 8, ch), F32),
            pltpu.VMEM((8, hid), F32),
            pltpu.VMEM((SMALL_TILES, 8, ch), F32),
            pltpu.VMEM((n_dev - 1, 8, ch), F32),
            pltpu.VMEM((8, ch), F32),
            pltpu.VMEM((SMALL_TILES, 8, ch), F32),
            pltpu.SemaphoreType.DMA((8,)),
            pltpu.SemaphoreType.DMA((8,)),
            pltpu.SemaphoreType.DMA((8,)),
            pltpu.SemaphoreType.DMA((8,)),
            pltpu.SemaphoreType.DMA,
            pltpu.SemaphoreType.DMA,
            pltpu.SemaphoreType.DMA,
            pltpu.SemaphoreType.DMA,
            pltpu.SemaphoreType.DMA((SMALL_TILES,)),
            pltpu.SemaphoreType.DMA,
            pltpu.SemaphoreType.DMA,
            pltpu.SemaphoreType.DMA((SMALL_TILES,)),
            pltpu.SemaphoreType.REGULAR,
        ],
        compiler_params=pltpu.CompilerParams(
            collective_id=0, has_side_effects=True, vmem_limit_bytes=48 << 20
        ),
    )(ocean_mask, *[pltpu.with_memory_space_constraint(x, pltpu.HBM) for x in operands])
    outs = store(outs)
    return (outs[0], outs[1], outs[2].transpose(0, 2, 1), outs[3], outs[4], outs[5].reshape(hid))


def solution(mesh):
    tiled = P("lat", "lon", None)
    placed = (tiled, tiled, P("lat", "lon")) + (P(),) * 9
    return jax.shard_map(
        functools.partial(body, (mesh.shape["lat"], mesh.shape["lon"])),
        mesh=mesh,
        in_specs=placed,
        out_specs=(tiled, tiled, P(None, "lat", "lon"), P(), P(), P()),
        check_vma=False,
    )
```

```python
import functools
import math

import jax
import jax.numpy as jnp
from jax import lax
from jax.experimental import pallas as pl
from jax.experimental.pallas import tpu as pltpu
from jax.sharding import PartitionSpec as P

GELU_COEF = 0.7978845608028654
MESH = pl.DeviceIdType.MESH
F32 = jnp.float32
BF16 = jnp.bfloat16
EDGE = 16
DIRS = [(a, b) for a in (-1, 0, 1) for b in (-1, 0, 1) if (a, b) != (0, 0)]
TAPS = 49
SMALL_TILES = 8


def gelu_pair(v):
    sq = v * v
    t = jnp.tanh(GELU_COEF * v * (1.0 + 0.044715 * sq))
    half = 0.5 * (1.0 + t)
    derivative = half + (0.5 * GELU_COEF) * v * (1.0 - t * t) * (1.0 + (3.0 * 0.044715) * sq)
    return v * half, derivative


def fold(x):
    return jnp.sum(x.reshape(x.shape[0] // 8, 8, x.shape[1]), axis=0)


def kernel(
    n_lat, n_lon, scale,
    mask, fields_hbm, *rest,
):
    sources, rest = (fields_hbm,) + rest[:10], rest[10:]
    block_out, grad_fields, grad_mlp, grad_kernel, grad_channels, grad_bias = rest[:6]
    cot, dk, dbias, gain, nbias, w_in, b_in, w_out, b_out, lscale = rest[6:16]
    (
    load_sem, pad, gpad, wide, xs, kb, ksum, dgrad, normed_s, gpre_s, hid_s, gout_s,
    packed, pair_recv, merged, mlp_recv, chan_acc, bias_acc, small, small_recv, small_sum, small_all,
    h_send, h_recv, g_send, g_recv, p_send, p_recv, m_send, m_recv, s_send, s_recv, a_send, a_recv, sync,
    ) = rest[16:]
    rows, cols, ch = cot.shape
    hid = w_in.shape[1]
    n_dev = n_lat * n_lon
    lat, lon = lax.axis_index("lat"), lax.axis_index("lon")
    me = lat * n_lon + lon
    per_lat = SMALL_TILES
    first_lon, lon_step = 0, 1

    def where(flat):
        return {"lat": flat // n_lon, "lon": flat % n_lon}

    barrier = pltpu.get_barrier_semaphore()

    def at(dlat, dlon):
        return {"lat": lat + dlat, "lon": (lon + dlon + n_lon) % n_lon}

    for dlat, dlon in DIRS:
        def greet():
            pl.semaphore_signal(barrier, inc=1, device_id=at(dlat, dlon), device_id_type=MESH)

        if dlat:
            pl.when((lat + dlat >= 0) & (lat + dlat < n_lat))(greet)
        else:
            greet()
    rows_beside = jnp.where(lat > 0, 1, 0) + jnp.where(lat < n_lat - 1, 1, 0)

    plane_size = 4 * n_lat - 1
    line_size = n_lon // 4 - 1

    def plane_signal(sem):
        @pl.loop(1, plane_size + 1)
        def _(k):
            place = (lat * 4 + lon % 4 + k) % (plane_size + 1)
            to = {"lat": place // 4, "lon": lon - lon % 4 + place % 4}
            pl.semaphore_signal(sem, inc=1, device_id=to, device_id_type=MESH)

    for k in range(1, line_size + 1):
        pl.semaphore_signal(barrier, inc=1, device_id=at(0, 4 * k), device_id_type=MESH)
    plane_signal(barrier)

    def halo(buf, send, recv, step, which=(-1, 0, 1)):
        cuts = {
            1: ((rows, rows + 3), (0, 3)),
            -1: ((3, 6), (rows + 3, rows + 6)),
            0: ((3, rows + 3), (3, rows + 3)),
        }
        cells = {
            1: ((cols, cols + EDGE), (0, EDGE)),
            -1: ((EDGE, 2 * EDGE), (cols + EDGE, cols + 2 * EDGE)),
            0: ((EDGE, cols + EDGE), (EDGE, cols + EDGE)),
        }
        for d, (dlat, dlon) in enumerate(DIRS):
            if dlat not in which:
                continue
            (s0, s1), (t0, t1) = cuts[dlat]
            (u0, u1), (v0, v1) = cells[dlon]
            copy = pltpu.make_async_remote_copy(
                src_ref=buf.at[pl.ds(s0, s1 - s0), pl.ds(u0, u1 - u0)],
                dst_ref=buf.at[pl.ds(t0, t1 - t0), pl.ds(v0, v1 - v0)],
                send_sem=send.at[d],
                recv_sem=recv.at[d],
                device_id={
                    "lat": lat + dlat,
                    "lon": (lon + dlon + n_lon) % n_lon,
                },
                device_id_type=MESH,
            )
            to = (lat + dlat >= 0) & (lat + dlat < n_lat)
            back = (lat - dlat >= 0) & (lat - dlat < n_lat)
            if step == "start":
                act, cond = copy.start, to
            elif step == "recv":
                act, cond = copy.wait_recv, back
            else:
                act, cond = copy.wait_send, to
            if dlat == 0:
                act()
            else:
                pl.when(cond)(act)

    center = pad.at[pl.ds(3, rows), pl.ds(EDGE, cols)]
    loads = [
        pltpu.make_async_copy(src, dst, load_sem.at[i])
        for i, (src, dst) in enumerate(zip(sources, (center,) + rest[6:16]))
    ]
    for load in loads:
        load.start()

    @pl.when(lat == 0)
    def _():
        pad[0:3] = jnp.zeros((3,) + pad.shape[1:], BF16)
        gpad[0:3] = jnp.zeros((3,) + pad.shape[1:], BF16)

    @pl.when(lat == n_lat - 1)
    def _():
        pad[rows + 3 : rows + 6] = jnp.zeros((3,) + pad.shape[1:], BF16)
        gpad[rows + 3 : rows + 6] = jnp.zeros((3,) + pad.shape[1:], BF16)

    chan_acc[...] = jnp.zeros(chan_acc.shape, F32)
    bias_acc[...] = jnp.zeros(bias_acc.shape, F32)
    small[SMALL_TILES - 1] = jnp.zeros((8, ch), F32)

    loads[0].wait()
    pl.semaphore_wait(barrier, 2 + 3 * rows_beside + line_size + plane_size)
    halo(pad, h_send, h_recv, "start")
    plane_signal(sync)
    for load in loads[1:]:
        load.wait()
    for a in range(7):
        for b in range(7):
            kb[a * 7 + b] = jnp.broadcast_to(dk[a, b : b + 1, :], (8, ch))

    def shifted(buf, start, stop):
        @pl.loop(start, stop)
        def _(r):
            wide[...] = buf[r].astype(F32)
            for b in range(7):
                xs[b, r] = wide[EDGE - 3 + b : EDGE - 3 + b + cols, :]

    def shifted_center(buf):
        @pl.loop(3, rows + 3)
        def _(r):
            wide[EDGE : EDGE + cols, :] = buf[r, EDGE : EDGE + cols, :].astype(F32)
            for b in range(7):
                xs[b, r, 8 : cols - 8, :] = wide[EDGE + 5 + b : EDGE + 5 + b + cols - 16, :]

    def shifted_ends(buf):
        @pl.loop(3, rows + 3)
        def _(r):
            wide[0 : 2 * EDGE, :] = buf[r, 0 : 2 * EDGE, :].astype(F32)
            wide[cols : cols + 2 * EDGE, :] = buf[r, cols : cols + 2 * EDGE, :].astype(F32)
            for b in range(7):
                xs[b, r, 0:8, :] = wide[EDGE - 3 + b : EDGE + 5 + b, :]
                xs[b, r, cols - 8 : cols, :] = wide[cols + EDGE - 11 + b : cols + EDGE - 3 + b, :]

    def chunk(j):
        return pl.ds(pl.multiple_of(j * 8, 8), 8)

    def stencil(j, flip, inputs, acc):
        acc = list(acc)
        for b in range(7):
            taps = [kb[TAPS - 1 - (a * 7 + b) if flip else a * 7 + b] for a in range(7)]
            for r in inputs:
                x = xs[b, r, chunk(j), :]
                for i in range(max(0, r - 6), min(rows, r + 1)):
                    term = taps[r - i] * x
                    acc[i] = term if acc[i] is None else acc[i] + term
        return acc

    inner = range(3, rows + 3)
    chunks = cols // 8
    some = rows // 2
    near = jnp.where(lat == 0, 0, some)
    far = some - near
    ocean = mask[0, 0].astype(F32)

    def whole_rows(j, flip, bias):
        for i, value in enumerate(stencil(j, flip, inner, [None] * rows)):
            dgrad[i, chunk(j), :] = value if bias is None else value + bias[...]

    def center(flip, bias, lo, hi):
        @pl.loop(lo, hi)
        def _(j):
            whole_rows(j, flip, bias)

    def ends_conv(buf, send, recv, flip, bias):
        halo(buf, send, recv, "recv", (0,))
        shifted_ends(buf)

        @pl.loop(0, 2)
        def _(k):
            whole_rows(k * (chunks - 1), flip, bias)

    def sides_conv(buf, send, recv, flip):
        halo(buf, send, recv, "recv", (-1, 1))

        def side(inputs):
            taken = [i for i in range(rows) if any(0 <= r - i < 7 for r in inputs)]
            shifted(buf, inputs[0], inputs[-1] + 1)

            @pl.loop(0, chunks // 2)
            def _(k):
                for j in (2 * k, 2 * k + 1):
                    start = [dgrad[i, chunk(j), :] if i in taken else None for i in range(rows)]
                    values = stencil(j, flip, inputs, start)
                    for i in taken:
                        dgrad[i, chunk(j), :] = values[i]

        pl.when(lat > 0)(functools.partial(side, range(3)))
        pl.when(lat < n_lat - 1)(functools.partial(side, range(rows + 3, rows + 6)))

    shifted_center(pad)
    center(False, dbias, 1, chunks - 1)

    def ends_first():
        ends_conv(pad, h_send, h_recv, False, dbias)

    def sides_first():
        sides_conv(pad, h_send, h_recv, False)

    def when_inside(step):
        if n_lat > 2:
            pl.when((lat > 0) & (lat < n_lat - 1))(step)

    def when_outside(step):
        if n_lat > 2:
            pl.when((lat == 0) | (lat == n_lat - 1))(step)
        else:
            step()

    def mlp(read, write, start, count):
        span = pl.ds(start, count)
        depth = read(dgrad, 0, 0)
        cot_rows = read(cot, 0, 0).astype(F32)
        centered = depth - jnp.sum(depth, axis=-1, keepdims=True) * (1.0 / ch)
        variance = jnp.sum(centered * centered, axis=-1, keepdims=True) * (1.0 / ch)
        inverse = lax.rsqrt(variance + 1e-06)
        normed = centered * inverse
        normed_low = (normed * gain[...] + nbias[...]).astype(BF16)
        pre = jnp.dot(normed_low, w_in[...], preferred_element_type=F32) + b_in[...]
        activated, derivative = gelu_pair(pre)
        hidden_low = activated.astype(BF16)
        out = jnp.dot(hidden_low, w_out[...], preferred_element_type=F32) + b_out[...]
        scaled = ocean * lscale[...]
        write(block_out, 0, 0, (read(pad, 3, EDGE).astype(F32) + scaled * out).astype(BF16))
        grad_out = scaled * cot_rows
        grad_out_low = grad_out.astype(BF16)
        nt = (((1,), (1,)), ((), ()))
        grad_hidden = lax.dot_general(grad_out_low, w_out[...], nt, preferred_element_type=F32)
        grad_pre = grad_hidden * derivative
        grad_pre_low = grad_pre.astype(BF16)
        grad_normed = lax.dot_general(grad_pre_low, w_in[...], nt, preferred_element_type=F32)
        grad_hat = grad_normed * gain[...]
        mean_hat = jnp.sum(grad_hat, axis=-1, keepdims=True) * (1.0 / ch)
        mean_dot = jnp.sum(grad_hat * normed, axis=-1, keepdims=True) * (1.0 / ch)
        grad_depth = inverse * (grad_hat - mean_hat - normed * mean_dot)
        write(dgrad, 0, 0, grad_depth)
        write(gpad, 3, EDGE, grad_depth.astype(BF16))
        normed_s[span, :] = normed_low
        gpre_s[span, :] = grad_pre_low
        hid_s[span, :] = hidden_low
        gout_s[span, :] = grad_out_low
        chan_acc[0] += fold(grad_depth)
        chan_acc[1] += fold(grad_normed * normed)
        chan_acc[2] += fold(grad_normed)
        chan_acc[3] += fold(grad_out)
        chan_acc[4] += fold(ocean * out * cot_rows)
        bias_acc[...] += fold(grad_pre)

    def strip(first, count, lo, hi):
        size = count * (hi - lo)

        def read(buf, above, before):
            return buf[pl.ds(above + first, count), before + lo : before + hi, :].reshape(size, ch)

        def write(buf, above, before, value):
            buf[pl.ds(above + first, count), before + lo : before + hi, :] = value.reshape(count, hi - lo, ch)

        return read, write

    def read_ends(buf, above, before):
        band = pl.ds(above + near, some)
        ends = [buf[band, before + c : before + c + 16, :] for c in (0, cols - 16)]
        return jnp.concatenate([end.reshape(some * 16, ch) for end in ends], axis=0)

    def write_ends(buf, above, before, value):
        band = pl.ds(above + near, some)
        for k, c in enumerate((0, cols - 16)):
            end = value[k * some * 16 : (k + 1) * some * 16]
            buf[band, before + c : before + c + 16, :] = end.reshape(some, 16, ch)

    def kernel_sums(b, first, js, sums):
        sums = list(sums)
        for j in js:
            x = xs[b, pl.ds(first, some + 6), chunk(j), :]
            g = dgrad[pl.ds(first, some), chunk(j), :]
            for a in range(7):
                sums[a] = sums[a] + jnp.sum(x[a : a + some] * g, axis=0)
        return tuple(sums)

    core = some * (cols - 32)
    ends = some * 32
    when_inside(ends_first)
    when_inside(sides_first)

    @pl.loop(0, some // 2)
    def _(t):
        mlp(*strip(near + 2 * t, 2, 16, cols - 16), pl.multiple_of(t * (core * 2 // some), 16), core * 2 // some)

    zero = jnp.zeros((8, ch), F32)
    for b in range(7):
        sums = lax.fori_loop(
            1, chunks // 2 - 1, lambda k, sums: kernel_sums(b, near, (2 * k, 2 * k + 1), sums), (zero,) * 7
        )
        for a in range(7):
            ksum[a * 7 + b] = sums[a]

    when_outside(ends_first)
    mlp(read_ends, write_ends, core, ends)
    for b in range(7):
        sums = tuple(ksum[a * 7 + b] for a in range(7))
        sums = kernel_sums(b, near, (0, 1, chunks - 2, chunks - 1), sums)
        for a in range(7):
            ksum[a * 7 + b] = sums[a]
    when_outside(sides_first)

    @pl.loop(0, some // 2)
    def _(t):
        mlp(*strip(far + 2 * t, 2, 0, cols), pl.multiple_of(core + ends + t * 2 * cols, 16), 2 * cols)

    halo(gpad, g_send, g_recv, "start")
    pl.semaphore_wait(sync, plane_size)

    for b in range(7):
        sums = tuple(ksum[a * 7 + b] for a in range(7))
        sums = lax.fori_loop(
            0, chunks // 2, lambda k, sums: kernel_sums(b, far, (2 * k, 2 * k + 1), sums), sums
        )
        for a in range(7):
            row = a * 7 + b
            small[row // 8, row % 8 : row % 8 + 1, :] = jnp.sum(sums[a], axis=0, keepdims=True)
    for i in range(5):
        row = TAPS + i
        small[row // 8, row % 8 : row % 8 + 1, :] = jnp.sum(chan_acc[i], axis=0, keepdims=True)
    bias_row = jnp.sum(bias_acc[...], axis=0, keepdims=True)
    for i in range(hid // ch):
        row = TAPS + 5 + i
        small[row // 8, row % 8 : row % 8 + 1, :] = bias_row[:, i * ch : (i + 1) * ch]

    def owner_of(t):
        return t // per_lat * n_lon + first_lon + t % per_lat * lon_step

    def small_copy(t):
        owner = owner_of(t)
        return pltpu.make_async_remote_copy(
            src_ref=small.at[t],
            dst_ref=small_recv.at[(owner - me - 1 + n_dev) % n_dev],
            send_sem=s_send.at[t],
            recv_sem=s_recv,
            device_id=where(owner),
            device_id_type=MESH,
        )

    for t in range(SMALL_TILES):

        @pl.when(me != owner_of(t))
        def _():
            small_copy(t).start()

    part = ch // n_lat
    units, half = hid // n_lon, n_lon // 2
    parity = lon % 2
    tt = (((0,), (0,)), ((), ()))
    win_t = lax.dot_general(normed_s[...], gpre_s[...], tt, preferred_element_type=F32).T
    wout_t = lax.dot_general(gout_s[...], hid_s[...], tt, preferred_element_type=F32).T
    lane = lax.broadcasted_iota(jnp.int32, (hid, ch), 1)
    for t in range(n_lat):
        first = pltpu.roll(win_t, (ch - part * t) % ch, 1) if t else win_t
        shift = (part - part * t) % ch
        second = pltpu.roll(wout_t, shift, 1) if shift else wout_t
        both = jnp.where(lane < part, first, second).astype(BF16)
        both = both.reshape(half, 2, units, ch)
        for q in range(2):
            packed[q, t] = both[:, q]

    pair = pltpu.make_async_remote_copy(
        src_ref=packed.at[1 - parity],
        dst_ref=pair_recv,
        send_sem=p_send,
        recv_sem=p_recv,
        device_id={"lat": lat, "lon": lon + 1 - 2 * parity},
        device_id_type=MESH,
    )
    pair.start()

    group = n_lat * half
    mine = lat * half + lon // 2

    def mlp_copy(k):
        to = (mine + 1 + k) % group
        return pltpu.make_async_remote_copy(
            src_ref=merged.at[to // half, to % half],
            dst_ref=mlp_recv.at[k],
            send_sem=m_send,
            recv_sem=m_recv,
            device_id={"lat": to // half, "lon": 2 * (to % half) + parity},
            device_id_type=MESH,
        )

    shifted_center(gpad)
    center(True, None, 1, chunks // 2)
    pair.wait_recv()
    merged[...] = (packed[parity].astype(F32) + pair_recv[...].astype(F32)).astype(BF16)

    @pl.loop(0, group - 1)
    def _(k):
        mlp_copy(k).start()

    center(True, None, chunks // 2, chunks - 1)

    tile = lat * per_lat + (lon - first_lon) // lon_step
    is_owner = (lat < SMALL_TILES // per_lat) & (lon >= first_lon) & (lon < first_lon + per_lat * lon_step)
    is_owner = is_owner & ((lon - first_lon) % lon_step == 0)

    def gather_copy(k):
        to = k + jnp.where(k >= me, 1, 0)
        return pltpu.make_async_remote_copy(
            src_ref=small_sum,
            dst_ref=small_all.at[tile],
            send_sem=a_send,
            recv_sem=a_recv.at[tile],
            device_id=where(to),
            device_id_type=MESH,
        )

    @pl.when(is_owner)
    def _():
        pltpu.make_async_copy(small_recv, small_recv, s_recv).wait()
        total = lax.fori_loop(0, n_dev - 1, lambda k, acc: acc + small_recv[k], small[tile])
        small_sum[...] = total * scale
        small_all[tile] = total * scale

        @pl.loop(0, n_dev - 1)
        def _(k):
            gather_copy(k).start()

    ends_conv(gpad, g_send, g_recv, True, None)
    sides_conv(gpad, g_send, g_recv, True)

    @pl.loop(0, rows)
    def _(i):
        grad_fields[i] = (cot[i].astype(F32) + dgrad[i]).astype(BF16)

    pltpu.make_async_copy(mlp_recv, mlp_recv, m_recv).wait()
    own = merged[lat, lon // 2].astype(F32)
    total = lax.fori_loop(0, group - 1, lambda k, acc: acc + mlp_recv[k].astype(F32), own)
    total = total * scale
    grad_mlp[0] = total[:, 0:part]
    grad_mlp[1] = total[:, part : 2 * part]

    for t in range(SMALL_TILES):

        @pl.when(me != owner_of(t))
        def _():
            pltpu.make_async_copy(small_sum, small_all.at[t], a_recv.at[t]).wait()

    for a in range(7):
        for b in range(7):
            row = a * 7 + b
            grad_kernel[a, b : b + 1, :] = small_all[row // 8, row % 8 : row % 8 + 1, :]
    for i in range(5):
        row = TAPS + i
        grad_channels[i : i + 1, :] = small_all[row // 8, row % 8 : row % 8 + 1, :]
    for i in range(hid // ch):
        row = TAPS + 5 + i
        grad_bias[:, i * ch : (i + 1) * ch] = small_all[row // 8, row % 8 : row % 8 + 1, :]

    halo(pad, h_send, h_recv, "sent")
    halo(gpad, g_send, g_recv, "sent")
    pair.wait_send()
    pltpu.make_async_copy(mlp_recv, mlp_recv, m_send).wait()
    for t in range(SMALL_TILES):

        @pl.when(me != owner_of(t))
        def _():
            small_copy(t).wait_send()

    @pl.when(is_owner)
    def _():
        pltpu.make_async_copy(small_recv, small_recv, a_send).wait()


def store_kernel(*refs):
    n = len(refs) // 2
    copies = [pltpu.make_async_copy(refs[i], refs[n + i], refs[-1].at[i]) for i in range(n)]
    for copy in copies:
        copy.start()
    for copy in copies:
        copy.wait()


def store(arrays):
    return pl.pallas_call(
        store_kernel,
        out_shape=[pltpu.HBM(x.shape, x.dtype) for x in arrays],
        in_specs=[pl.BlockSpec(memory_space=pltpu.VMEM)] * len(arrays),
        out_specs=[pl.BlockSpec(memory_space=pltpu.HBM)] * len(arrays),
        scratch_shapes=[pltpu.SemaphoreType.DMA((len(arrays),))],
    )(*[pltpu.with_memory_space_constraint(x, pltpu.VMEM) for x in arrays])


def body(mesh_shape, fields, cotangent, ocean_mask, depth_kernel, depth_bias, norm_gain, norm_bias,
         weight_in, bias_in, weight_out, bias_out, layer_scale):
    n_lat, n_lon = mesh_shape
    n_dev = n_lat * n_lon
    rows, cols, ch = fields.shape
    hid = weight_in.shape[1]
    units, part, cells = hid // n_lon, ch // n_lat, rows * cols
    scale = 1.0 / math.sqrt(cells * n_dev)
    vmem = pl.BlockSpec(memory_space=pltpu.VMEM)
    shares = (n_lat, n_lon // 2, units, ch)
    padded = (rows + 6, cols + 2 * EDGE, ch)
    operands = (
        fields, cotangent, depth_kernel, depth_bias.reshape(1, ch), norm_gain.reshape(1, ch),
        norm_bias.reshape(1, ch), weight_in, bias_in.reshape(1, hid), weight_out,
        bias_out.reshape(1, ch), layer_scale.reshape(1, ch),
    )
    outs = pl.pallas_call(
        functools.partial(kernel, n_lat, n_lon, scale),
        out_shape=[
            jax.ShapeDtypeStruct(fields.shape, BF16),
            jax.ShapeDtypeStruct(fields.shape, BF16),
            jax.ShapeDtypeStruct((2, units, part), F32),
            jax.ShapeDtypeStruct((7, 7, ch), F32),
            jax.ShapeDtypeStruct((5, ch), F32),
            jax.ShapeDtypeStruct((1, hid), F32),
        ],
        in_specs=[pl.BlockSpec(memory_space=pltpu.SMEM)] + [pl.BlockSpec(memory_space=pltpu.HBM)] * 11,
        out_specs=[vmem] * 6,
        scratch_shapes=[pltpu.VMEM(x.shape, x.dtype) for x in operands[1:]]
        + [
            pltpu.SemaphoreType.DMA((11,)),
            pltpu.VMEM(padded, BF16),
            pltpu.VMEM(padded, BF16),
            pltpu.VMEM(padded[1:], F32),
            pltpu.VMEM((7, rows + 6, cols, ch), F32),
            pltpu.VMEM((TAPS, 8, ch), F32),
            pltpu.VMEM((TAPS, 8, ch), F32),
            pltpu.VMEM((rows, cols, ch), F32),
            pltpu.VMEM((cells, ch), BF16),
            pltpu.VMEM((cells, hid), BF16),
            pltpu.VMEM((cells, hid), BF16),
            pltpu.VMEM((cells, ch), BF16),
            pltpu.VMEM((2,) + shares, BF16),
            pltpu.VMEM(shares, BF16),
            pltpu.VMEM(shares, BF16),
            pltpu.VMEM((n_dev // 2 - 1, units, ch), BF16),
            pltpu.VMEM((5, 8, ch), F32),
            pltpu.VMEM((8, hid), F32),
            pltpu.VMEM((SMALL_TILES, 8, ch), F32),
            pltpu.VMEM((n_dev - 1, 8, ch), F32),
            pltpu.VMEM((8, ch), F32),
            pltpu.VMEM((SMALL_TILES, 8, ch), F32),
            pltpu.SemaphoreType.DMA((8,)),
            pltpu.SemaphoreType.DMA((8,)),
            pltpu.SemaphoreType.DMA((8,)),
            pltpu.SemaphoreType.DMA((8,)),
            pltpu.SemaphoreType.DMA,
            pltpu.SemaphoreType.DMA,
            pltpu.SemaphoreType.DMA,
            pltpu.SemaphoreType.DMA,
            pltpu.SemaphoreType.DMA((SMALL_TILES,)),
            pltpu.SemaphoreType.DMA,
            pltpu.SemaphoreType.DMA,
            pltpu.SemaphoreType.DMA((SMALL_TILES,)),
            pltpu.SemaphoreType.REGULAR,
        ],
        compiler_params=pltpu.CompilerParams(
            collective_id=0, has_side_effects=True, vmem_limit_bytes=48 << 20
        ),
    )(ocean_mask, *[pltpu.with_memory_space_constraint(x, pltpu.HBM) for x in operands])
    outs = store(outs)
    return (outs[0], outs[1], outs[2].transpose(0, 2, 1), outs[3], outs[4], outs[5].reshape(hid))


def solution(mesh):
    tiled = P("lat", "lon", None)
    placed = (tiled, tiled, P("lat", "lon")) + (P(),) * 9
    return jax.shard_map(
        functools.partial(body, (mesh.shape["lat"], mesh.shape["lon"])),
        mesh=mesh,
        in_specs=placed,
        out_specs=(tiled, tiled, P(None, "lat", "lon"), P(), P(), P()),
        check_vma=False,
    )
```

```python
import functools
import math

import jax
import jax.numpy as jnp
from jax import lax
from jax.experimental import pallas as pl
from jax.experimental.pallas import tpu as pltpu
from jax.sharding import PartitionSpec as P

GELU_COEF = 0.7978845608028654
MESH = pl.DeviceIdType.MESH
F32 = jnp.float32
BF16 = jnp.bfloat16
EDGE = 16
DIRS = [(a, b) for a in (-1, 0, 1) for b in (-1, 0, 1) if (a, b) != (0, 0)]
TAPS = 49
SMALL_TILES = 8


def gelu_pair(v):
    sq = v * v
    half = 0.5 + 0.5 * jnp.tanh(v * (GELU_COEF + (0.044715 * GELU_COEF) * sq))
    activated = v * half
    slope = (1.0 - half) * (2.0 * GELU_COEF + (6.0 * 0.044715 * GELU_COEF) * sq)
    return activated, half + activated * slope


def fold(x):
    return jnp.sum(x.reshape(x.shape[0] // 8, 8, x.shape[1]), axis=0)


def tree(terms):
    while len(terms) > 1:
        pairs = [terms[k] + terms[k + 1] for k in range(0, len(terms) - 1, 2)]
        terms = pairs + terms[len(terms) - len(terms) % 2 :]
    return terms[0]


def kernel(
    n_lat, n_lon, scale,
    mask, fields_hbm, *rest,
):
    sources, rest = (fields_hbm,) + rest[:10], rest[10:]
    block_out, grad_fields, grad_mlp, grad_kernel, grad_channels, grad_bias = rest[:6]
    cot, dk, dbias, gain, nbias, w_in, b_in, w_out, b_out, lscale = rest[6:16]
    (
    load_sem, pad, gpad, wide, xs, kb, ksum, dgrad, normed_s, gpre_s, hid_s, gout_s,
    packed, pair_recv, merged, mlp_recv, chan_acc, bias_acc, small, small_recv, small_sum, small_all,
    h_send, h_recv, g_send, g_recv, p_send, p_recv, m_send, m_recv, s_send, s_recv, a_send, a_recv, sync,
    ) = rest[16:]
    rows, cols, ch = cot.shape
    hid = w_in.shape[1]
    n_dev = n_lat * n_lon
    lat, lon = lax.axis_index("lat"), lax.axis_index("lon")
    me = lat * n_lon + lon
    per_lat = SMALL_TILES
    first_lon, lon_step = 0, 1

    def where(flat):
        return {"lat": flat // n_lon, "lon": flat % n_lon}

    barrier = pltpu.get_barrier_semaphore()

    def at(dlat, dlon):
        return {"lat": lat + dlat, "lon": (lon + dlon + n_lon) % n_lon}

    for dlat, dlon in DIRS:
        def greet():
            pl.semaphore_signal(barrier, inc=1, device_id=at(dlat, dlon), device_id_type=MESH)

        if dlat:
            pl.when((lat + dlat >= 0) & (lat + dlat < n_lat))(greet)
        else:
            greet()
    rows_beside = jnp.where(lat > 0, 1, 0) + jnp.where(lat < n_lat - 1, 1, 0)

    plane_size = 4 * n_lat - 1
    line_size = n_lon // 4 - 1

    def plane_signal(sem):
        @pl.loop(1, plane_size + 1)
        def _(k):
            place = (lat * 4 + lon % 4 + k) % (plane_size + 1)
            to = {"lat": place // 4, "lon": lon - lon % 4 + place % 4}
            pl.semaphore_signal(sem, inc=1, device_id=to, device_id_type=MESH)

    for k in range(1, line_size + 1):
        pl.semaphore_signal(barrier, inc=1, device_id=at(0, 4 * k), device_id_type=MESH)
    plane_signal(barrier)

    def halo(buf, send, recv, step, which=(-1, 0, 1)):
        cuts = {
            1: ((rows, rows + 3), (0, 3)),
            -1: ((3, 6), (rows + 3, rows + 6)),
            0: ((3, rows + 3), (3, rows + 3)),
        }
        cells = {
            1: ((cols, cols + EDGE), (0, EDGE)),
            -1: ((EDGE, 2 * EDGE), (cols + EDGE, cols + 2 * EDGE)),
            0: ((EDGE, cols + EDGE), (EDGE, cols + EDGE)),
        }
        for d, (dlat, dlon) in enumerate(DIRS):
            if dlat not in which:
                continue
            (s0, s1), (t0, t1) = cuts[dlat]
            (u0, u1), (v0, v1) = cells[dlon]
            copy = pltpu.make_async_remote_copy(
                src_ref=buf.at[pl.ds(s0, s1 - s0), pl.ds(u0, u1 - u0)],
                dst_ref=buf.at[pl.ds(t0, t1 - t0), pl.ds(v0, v1 - v0)],
                send_sem=send.at[d],
                recv_sem=recv.at[d],
                device_id={
                    "lat": lat + dlat,
                    "lon": (lon + dlon + n_lon) % n_lon,
                },
                device_id_type=MESH,
            )
            to = (lat + dlat >= 0) & (lat + dlat < n_lat)
            back = (lat - dlat >= 0) & (lat - dlat < n_lat)
            if step == "start":
                act, cond = copy.start, to
            elif step == "recv":
                act, cond = copy.wait_recv, back
            else:
                act, cond = copy.wait_send, to
            if dlat == 0:
                act()
            else:
                pl.when(cond)(act)

    center = pad.at[pl.ds(3, rows), pl.ds(EDGE, cols)]
    loads = [
        pltpu.make_async_copy(src, dst, load_sem.at[i])
        for i, (src, dst) in enumerate(zip(sources, (center,) + rest[6:16]))
    ]
    for load in loads:
        load.start()

    @pl.when(lat == 0)
    def _():
        pad[0:3] = jnp.zeros((3,) + pad.shape[1:], BF16)
        gpad[0:3] = jnp.zeros((3,) + pad.shape[1:], BF16)

    @pl.when(lat == n_lat - 1)
    def _():
        pad[rows + 3 : rows + 6] = jnp.zeros((3,) + pad.shape[1:], BF16)
        gpad[rows + 3 : rows + 6] = jnp.zeros((3,) + pad.shape[1:], BF16)

    chan_acc[...] = jnp.zeros(chan_acc.shape, F32)
    bias_acc[...] = jnp.zeros(bias_acc.shape, F32)
    small[SMALL_TILES - 1] = jnp.zeros((8, ch), F32)

    loads[0].wait()
    pl.semaphore_wait(barrier, 2 + 3 * rows_beside + line_size + plane_size)
    halo(pad, h_send, h_recv, "start")
    plane_signal(sync)
    for load in loads[1:]:
        load.wait()
    for a in range(7):
        for b in range(7):
            kb[a * 7 + b] = jnp.broadcast_to(dk[a, b : b + 1, :], (8, ch))

    def shifted(buf, start, stop):
        @pl.loop(start, stop)
        def _(r):
            wide[...] = buf[r].astype(F32)
            for b in range(7):
                xs[b, r] = wide[EDGE - 3 + b : EDGE - 3 + b + cols, :]

    def shifted_center(buf):
        @pl.loop(3, rows + 3)
        def _(r):
            wide[EDGE : EDGE + cols, :] = buf[r, EDGE : EDGE + cols, :].astype(F32)
            for b in range(7):
                xs[b, r, 8 : cols - 8, :] = wide[EDGE + 5 + b : EDGE + 5 + b + cols - 16, :]

    def shifted_ends(buf):
        @pl.loop(3, rows + 3)
        def _(r):
            wide[0 : 2 * EDGE, :] = buf[r, 0 : 2 * EDGE, :].astype(F32)
            wide[cols : cols + 2 * EDGE, :] = buf[r, cols : cols + 2 * EDGE, :].astype(F32)
            for b in range(7):
                xs[b, r, 0:8, :] = wide[EDGE - 3 + b : EDGE + 5 + b, :]
                xs[b, r, cols - 8 : cols, :] = wide[cols + EDGE - 11 + b : cols + EDGE - 3 + b, :]

    def chunk(j):
        return pl.ds(pl.multiple_of(j * 8, 8), 8)

    def stencil(j, flip, inputs, acc):
        acc = list(acc)
        for b in range(7):
            taps = [kb[TAPS - 1 - (a * 7 + b) if flip else a * 7 + b] for a in range(7)]
            for r in inputs:
                x = xs[b, r, chunk(j), :]
                for i in range(max(0, r - 6), min(rows, r + 1)):
                    term = taps[r - i] * x
                    acc[i] = term if acc[i] is None else acc[i] + term
        return acc

    inner = range(3, rows + 3)
    chunks = cols // 8
    some = rows // 2
    near = jnp.where(lat == 0, 0, some)
    far = some - near
    ocean = mask[0, 0].astype(F32)

    def whole_rows(j, flip, bias):
        for i, value in enumerate(stencil(j, flip, inner, [None] * rows)):
            dgrad[i, chunk(j), :] = value if bias is None else value + bias[...]

    def center(flip, bias, lo, hi):
        @pl.loop(lo, hi)
        def _(j):
            whole_rows(j, flip, bias)

    def ends_conv(buf, send, recv, flip, bias):
        halo(buf, send, recv, "recv", (0,))
        shifted_ends(buf)

        @pl.loop(0, 2)
        def _(k):
            whole_rows(k * (chunks - 1), flip, bias)

    def sides_conv(buf, send, recv, flip):
        halo(buf, send, recv, "recv", (-1, 1))

        def side(inputs):
            taken = [i for i in range(rows) if any(0 <= r - i < 7 for r in inputs)]
            shifted(buf, inputs[0], inputs[-1] + 1)

            @pl.loop(0, chunks // 2)
            def _(k):
                for j in (2 * k, 2 * k + 1):
                    start = [dgrad[i, chunk(j), :] if i in taken else None for i in range(rows)]
                    values = stencil(j, flip, inputs, start)
                    for i in taken:
                        dgrad[i, chunk(j), :] = values[i]

        pl.when(lat > 0)(functools.partial(side, range(3)))
        pl.when(lat < n_lat - 1)(functools.partial(side, range(rows + 3, rows + 6)))

    shifted_center(pad)
    center(False, dbias, 1, chunks - 1)

    def ends_first():
        ends_conv(pad, h_send, h_recv, False, dbias)

    def sides_first():
        sides_conv(pad, h_send, h_recv, False)

    def when_inside(step):
        if n_lat > 2:
            pl.when((lat > 0) & (lat < n_lat - 1))(step)

    def when_outside(step):
        if n_lat > 2:
            pl.when((lat == 0) | (lat == n_lat - 1))(step)
        else:
            step()

    def mlp(read, write, start, count):
        span = pl.ds(start, count)
        depth = read(dgrad, 0, 0)
        cot_rows = read(cot, 0, 0).astype(F32)
        centered = depth - jnp.sum(depth, axis=-1, keepdims=True) * (1.0 / ch)
        variance = jnp.sum(centered * centered, axis=-1, keepdims=True) * (1.0 / ch)
        inverse = lax.rsqrt(variance + 1e-06)
        normed = centered * inverse
        normed_low = (normed * gain[...] + nbias[...]).astype(BF16)
        pre = jnp.dot(normed_low, w_in[...], preferred_element_type=F32) + b_in[...]
        activated, derivative = gelu_pair(pre)
        hidden_low = activated.astype(BF16)
        out = jnp.dot(hidden_low, w_out[...], preferred_element_type=F32) + b_out[...]
        scaled = ocean * lscale[...]
        write(block_out, 0, 0, (read(pad, 3, EDGE).astype(F32) + scaled * out).astype(BF16))
        grad_out = scaled * cot_rows
        grad_out_low = grad_out.astype(BF16)
        nt = (((1,), (1,)), ((), ()))
        grad_hidden = lax.dot_general(grad_out_low, w_out[...], nt, preferred_element_type=F32)
        grad_pre = grad_hidden * derivative
        grad_pre_low = grad_pre.astype(BF16)
        grad_normed = lax.dot_general(grad_pre_low, w_in[...], nt, preferred_element_type=F32)
        grad_hat = grad_normed * gain[...]
        mean_hat = jnp.sum(grad_hat, axis=-1, keepdims=True) * (1.0 / ch)
        mean_dot = jnp.sum(grad_hat * normed, axis=-1, keepdims=True) * (1.0 / ch)
        grad_depth = inverse * (grad_hat - mean_hat - normed * mean_dot)
        write(dgrad, 0, 0, grad_depth)
        write(gpad, 3, EDGE, grad_depth.astype(BF16))
        normed_s[span, :] = normed_low
        gpre_s[span, :] = grad_pre_low
        hid_s[span, :] = hidden_low
        gout_s[span, :] = grad_out_low
        chan_acc[0] += fold(grad_depth)
        chan_acc[1] += fold(grad_normed * normed)
        chan_acc[2] += fold(grad_normed)
        chan_acc[3] += fold(grad_out)
        chan_acc[4] += fold(ocean * out * cot_rows)
        bias_acc[...] += fold(grad_pre)

    def strip(first, count, lo, hi):
        size = count * (hi - lo)

        def read(buf, above, before):
            return buf[pl.ds(above + first, count), before + lo : before + hi, :].reshape(size, ch)

        def write(buf, above, before, value):
            buf[pl.ds(above + first, count), before + lo : before + hi, :] = value.reshape(count, hi - lo, ch)

        return read, write

    def read_ends(buf, above, before):
        band = pl.ds(above + near, some)
        ends = [buf[band, before + c : before + c + 16, :] for c in (0, cols - 16)]
        return jnp.concatenate([end.reshape(some * 16, ch) for end in ends], axis=0)

    def write_ends(buf, above, before, value):
        band = pl.ds(above + near, some)
        for k, c in enumerate((0, cols - 16)):
            end = value[k * some * 16 : (k + 1) * some * 16]
            buf[band, before + c : before + c + 16, :] = end.reshape(some, 16, ch)

    def kernel_sums(b, first, blocks, sums):
        x, g = [], []
        for k in blocks:
            cells = pl.ds(pl.multiple_of(k * 16, 16), 16)
            x.append([xs[b, first + r, cells, :].astype(BF16) for r in range(some + 6)])
            g.append([dgrad[first + i, cells, :].astype(BF16) for i in range(some)])
        sums = list(sums)
        for a in range(7):
            low = tree([x[k][a + i] * g[k][i] for k in range(len(blocks)) for i in range(some)]).astype(F32)
            sums[a] = sums[a] + (low[0:8] + low[8:16])
        return tuple(sums)

    core = some * (cols - 32)
    ends = some * 32
    when_inside(ends_first)
    when_inside(sides_first)

    @pl.loop(0, some // 2)
    def _(t):
        mlp(*strip(near + 2 * t, 2, 16, cols - 16), pl.multiple_of(t * (core * 2 // some), 16), core * 2 // some)

    zero = jnp.zeros((8, ch), F32)
    for b in range(7):
        sums = lax.fori_loop(
            0, chunks // 4 - 1, lambda k, sums: kernel_sums(b, near, (2 * k + 1, 2 * k + 2), sums), (zero,) * 7
        )
        for a in range(7):
            ksum[a * 7 + b] = sums[a]

    when_outside(ends_first)
    mlp(read_ends, write_ends, core, ends)
    for b in range(7):
        sums = tuple(ksum[a * 7 + b] for a in range(7))
        sums = kernel_sums(b, near, (0, chunks // 2 - 1), sums)
        for a in range(7):
            ksum[a * 7 + b] = sums[a]
    when_outside(sides_first)

    @pl.loop(0, some // 2)
    def _(t):
        mlp(*strip(far + 2 * t, 2, 0, cols), pl.multiple_of(core + ends + t * 2 * cols, 16), 2 * cols)

    pl.semaphore_wait(sync, plane_size)

    for b in range(7):
        sums = tuple(ksum[a * 7 + b] for a in range(7))
        sums = lax.fori_loop(
            0, chunks // 4, lambda k, sums: kernel_sums(b, far, (2 * k, 2 * k + 1), sums), sums
        )
        for a in range(7):
            row = a * 7 + b
            small[row // 8, row % 8 : row % 8 + 1, :] = jnp.sum(sums[a], axis=0, keepdims=True)
    for i in range(5):
        row = TAPS + i
        small[row // 8, row % 8 : row % 8 + 1, :] = jnp.sum(chan_acc[i], axis=0, keepdims=True)
    bias_row = jnp.sum(bias_acc[...], axis=0, keepdims=True)
    for i in range(hid // ch):
        row = TAPS + 5 + i
        small[row // 8, row % 8 : row % 8 + 1, :] = bias_row[:, i * ch : (i + 1) * ch]

    def owner_of(t):
        return t // per_lat * n_lon + first_lon + t % per_lat * lon_step

    def small_copy(t):
        owner = owner_of(t)
        return pltpu.make_async_remote_copy(
            src_ref=small.at[t],
            dst_ref=small_recv.at[(owner - me - 1 + n_dev) % n_dev],
            send_sem=s_send.at[t],
            recv_sem=s_recv,
            device_id=where(owner),
            device_id_type=MESH,
        )

    for t in range(SMALL_TILES):

        @pl.when(me != owner_of(t))
        def _():
            small_copy(t).start()

    halo(gpad, g_send, g_recv, "start")

    part = ch // n_lat
    units, half = hid // n_lon, n_lon // 2
    parity = lon % 2
    tt = (((0,), (0,)), ((), ()))
    win_t = lax.dot_general(normed_s[...], gpre_s[...], tt, preferred_element_type=F32).T
    wout_t = lax.dot_general(gout_s[...], hid_s[...], tt, preferred_element_type=F32).T
    lane = lax.broadcasted_iota(jnp.int32, (hid, ch), 1)
    for t in range(n_lat):
        first = pltpu.roll(win_t, (ch - part * t) % ch, 1) if t else win_t
        shift = (part - part * t) % ch
        second = pltpu.roll(wout_t, shift, 1) if shift else wout_t
        both = jnp.where(lane < part, first, second).astype(BF16)
        both = both.reshape(half, 2, units, ch)
        for q in range(2):
            packed[q, t] = both[:, q]

    pair = pltpu.make_async_remote_copy(
        src_ref=packed.at[1 - parity],
        dst_ref=pair_recv,
        send_sem=p_send,
        recv_sem=p_recv,
        device_id={"lat": lat, "lon": lon + 1 - 2 * parity},
        device_id_type=MESH,
    )
    pair.start()

    group = n_lat * half
    mine = lat * half + lon // 2

    def mlp_copy(k):
        to = (mine + 1 + k) % group
        return pltpu.make_async_remote_copy(
            src_ref=merged.at[to // half, to % half],
            dst_ref=mlp_recv.at[k],
            send_sem=m_send,
            recv_sem=m_recv,
            device_id={"lat": to // half, "lon": 2 * (to % half) + parity},
            device_id_type=MESH,
        )

    shifted_center(gpad)
    center(True, None, 1, chunks // 2)
    pair.wait_recv()
    merged[...] = (packed[parity].astype(F32) + pair_recv[...].astype(F32)).astype(BF16)

    @pl.loop(0, group - 1)
    def _(k):
        mlp_copy(k).start()

    center(True, None, chunks // 2, chunks - 1)

    tile = lat * per_lat + (lon - first_lon) // lon_step
    is_owner = (lat < SMALL_TILES // per_lat) & (lon >= first_lon) & (lon < first_lon + per_lat * lon_step)
    is_owner = is_owner & ((lon - first_lon) % lon_step == 0)

    def gather_copy(k):
        to = k + jnp.where(k >= me, 1, 0)
        return pltpu.make_async_remote_copy(
            src_ref=small_sum,
            dst_ref=small_all.at[tile],
            send_sem=a_send,
            recv_sem=a_recv.at[tile],
            device_id=where(to),
            device_id_type=MESH,
        )

    @pl.when(is_owner)
    def _():
        pltpu.make_async_copy(small_recv, small_recv, s_recv).wait()
        total = lax.fori_loop(0, n_dev - 1, lambda k, acc: acc + small_recv[k], small[tile])
        small_sum[...] = total * scale
        small_all[tile] = total * scale

        @pl.loop(0, n_dev - 1)
        def _(k):
            gather_copy(k).start()

    ends_conv(gpad, g_send, g_recv, True, None)
    sides_conv(gpad, g_send, g_recv, True)

    @pl.loop(0, rows)
    def _(i):
        grad_fields[i] = (cot[i].astype(F32) + dgrad[i]).astype(BF16)

    pltpu.make_async_copy(mlp_recv, mlp_recv, m_recv).wait()
    own = merged[lat, lon // 2].astype(F32)
    total = lax.fori_loop(0, group - 1, lambda k, acc: acc + mlp_recv[k].astype(F32), own)
    total = total * scale
    grad_mlp[0] = total[:, 0:part]
    grad_mlp[1] = total[:, part : 2 * part]

    for t in range(SMALL_TILES):

        @pl.when(me != owner_of(t))
        def _():
            pltpu.make_async_copy(small_sum, small_all.at[t], a_recv.at[t]).wait()

    for a in range(7):
        for b in range(7):
            row = a * 7 + b
            grad_kernel[a, b : b + 1, :] = small_all[row // 8, row % 8 : row % 8 + 1, :]
    for i in range(5):
        row = TAPS + i
        grad_channels[i : i + 1, :] = small_all[row // 8, row % 8 : row % 8 + 1, :]
    for i in range(hid // ch):
        row = TAPS + 5 + i
        grad_bias[:, i * ch : (i + 1) * ch] = small_all[row // 8, row % 8 : row % 8 + 1, :]

    halo(pad, h_send, h_recv, "sent")
    halo(gpad, g_send, g_recv, "sent")
    pair.wait_send()
    pltpu.make_async_copy(mlp_recv, mlp_recv, m_send).wait()
    for t in range(SMALL_TILES):

        @pl.when(me != owner_of(t))
        def _():
            small_copy(t).wait_send()

    @pl.when(is_owner)
    def _():
        pltpu.make_async_copy(small_recv, small_recv, a_send).wait()


def store_kernel(*refs):
    n = len(refs) // 2
    copies = [pltpu.make_async_copy(refs[i], refs[n + i], refs[-1].at[i]) for i in range(n)]
    for copy in copies:
        copy.start()
    for copy in copies:
        copy.wait()


def store(arrays):
    return pl.pallas_call(
        store_kernel,
        out_shape=[pltpu.HBM(x.shape, x.dtype) for x in arrays],
        in_specs=[pl.BlockSpec(memory_space=pltpu.VMEM)] * len(arrays),
        out_specs=[pl.BlockSpec(memory_space=pltpu.HBM)] * len(arrays),
        scratch_shapes=[pltpu.SemaphoreType.DMA((len(arrays),))],
    )(*[pltpu.with_memory_space_constraint(x, pltpu.VMEM) for x in arrays])


def body(mesh_shape, fields, cotangent, ocean_mask, depth_kernel, depth_bias, norm_gain, norm_bias,
         weight_in, bias_in, weight_out, bias_out, layer_scale):
    n_lat, n_lon = mesh_shape
    n_dev = n_lat * n_lon
    rows, cols, ch = fields.shape
    hid = weight_in.shape[1]
    units, part, cells = hid // n_lon, ch // n_lat, rows * cols
    scale = 1.0 / math.sqrt(cells * n_dev)
    vmem = pl.BlockSpec(memory_space=pltpu.VMEM)
    shares = (n_lat, n_lon // 2, units, ch)
    padded = (rows + 6, cols + 2 * EDGE, ch)
    operands = (
        fields, cotangent, depth_kernel, depth_bias.reshape(1, ch), norm_gain.reshape(1, ch),
        norm_bias.reshape(1, ch), weight_in, bias_in.reshape(1, hid), weight_out,
        bias_out.reshape(1, ch), layer_scale.reshape(1, ch),
    )
    outs = pl.pallas_call(
        functools.partial(kernel, n_lat, n_lon, scale),
        out_shape=[
            jax.ShapeDtypeStruct(fields.shape, BF16),
            jax.ShapeDtypeStruct(fields.shape, BF16),
            jax.ShapeDtypeStruct((2, units, part), F32),
            jax.ShapeDtypeStruct((7, 7, ch), F32),
            jax.ShapeDtypeStruct((5, ch), F32),
            jax.ShapeDtypeStruct((1, hid), F32),
        ],
        in_specs=[pl.BlockSpec(memory_space=pltpu.SMEM)] + [pl.BlockSpec(memory_space=pltpu.HBM)] * 11,
        out_specs=[vmem] * 6,
        scratch_shapes=[pltpu.VMEM(x.shape, x.dtype) for x in operands[1:]]
        + [
            pltpu.SemaphoreType.DMA((11,)),
            pltpu.VMEM(padded, BF16),
            pltpu.VMEM(padded, BF16),
            pltpu.VMEM(padded[1:], F32),
            pltpu.VMEM((7, rows + 6, cols, ch), F32),
            pltpu.VMEM((TAPS, 8, ch), F32),
            pltpu.VMEM((TAPS, 8, ch), F32),
            pltpu.VMEM((rows, cols, ch), F32),
            pltpu.VMEM((cells, ch), BF16),
            pltpu.VMEM((cells, hid), BF16),
            pltpu.VMEM((cells, hid), BF16),
            pltpu.VMEM((cells, ch), BF16),
            pltpu.VMEM((2,) + shares, BF16),
            pltpu.VMEM(shares, BF16),
            pltpu.VMEM(shares, BF16),
            pltpu.VMEM((n_dev // 2 - 1, units, ch), BF16),
            pltpu.VMEM((5, 8, ch), F32),
            pltpu.VMEM((8, hid), F32),
            pltpu.VMEM((SMALL_TILES, 8, ch), F32),
            pltpu.VMEM((n_dev - 1, 8, ch), F32),
            pltpu.VMEM((8, ch), F32),
            pltpu.VMEM((SMALL_TILES, 8, ch), F32),
            pltpu.SemaphoreType.DMA((8,)),
            pltpu.SemaphoreType.DMA((8,)),
            pltpu.SemaphoreType.DMA((8,)),
            pltpu.SemaphoreType.DMA((8,)),
            pltpu.SemaphoreType.DMA,
            pltpu.SemaphoreType.DMA,
            pltpu.SemaphoreType.DMA,
            pltpu.SemaphoreType.DMA,
            pltpu.SemaphoreType.DMA((SMALL_TILES,)),
            pltpu.SemaphoreType.DMA,
            pltpu.SemaphoreType.DMA,
            pltpu.SemaphoreType.DMA((SMALL_TILES,)),
            pltpu.SemaphoreType.REGULAR,
        ],
        compiler_params=pltpu.CompilerParams(
            collective_id=0, has_side_effects=True, vmem_limit_bytes=48 << 20
        ),
    )(ocean_mask, *[pltpu.with_memory_space_constraint(x, pltpu.HBM) for x in operands])
    outs = store(outs)
    return (outs[0], outs[1], outs[2].transpose(0, 2, 1), outs[3], outs[4], outs[5].reshape(hid))


def solution(mesh):
    tiled = P("lat", "lon", None)
    placed = (tiled, tiled, P("lat", "lon")) + (P(),) * 9
    return jax.shard_map(
        functools.partial(body, (mesh.shape["lat"], mesh.shape["lon"])),
        mesh=mesh,
        in_specs=placed,
        out_specs=(tiled, tiled, P(None, "lat", "lon"), P(), P(), P()),
        check_vma=False,
    )
```

```python
import functools
import math

import jax
import jax.numpy as jnp
from jax import lax
from jax.experimental import pallas as pl
from jax.experimental.pallas import tpu as pltpu
from jax.sharding import PartitionSpec as P

GELU_COEF = 0.7978845608028654
MESH = pl.DeviceIdType.MESH
F32 = jnp.float32
BF16 = jnp.bfloat16
EDGE = 16
DIRS = [(a, b) for a in (-1, 0, 1) for b in (-1, 0, 1) if (a, b) != (0, 0)]
TAPS = 49
SMALL_TILES = 8


def gelu_pair(v):
    sq = v * v
    half = 0.5 + 0.5 * jnp.tanh(v * (GELU_COEF + (0.044715 * GELU_COEF) * sq))
    activated = v * half
    slope = (1.0 - half) * (2.0 * GELU_COEF + (6.0 * 0.044715 * GELU_COEF) * sq)
    return activated, half + activated * slope


def fold(x):
    return jnp.sum(x.reshape(x.shape[0] // 8, 8, x.shape[1]), axis=0)


def tree(terms):
    while len(terms) > 1:
        pairs = [terms[k] + terms[k + 1] for k in range(0, len(terms) - 1, 2)]
        terms = pairs + terms[len(terms) - len(terms) % 2 :]
    return terms[0]


def kernel(
    n_lat, n_lon, scale,
    mask, fields_hbm, *rest,
):
    sources, rest = (fields_hbm,) + rest[:10], rest[10:]
    block_out, grad_fields, grad_mlp, grad_kernel, grad_channels, grad_bias = rest[:6]
    cot, dk, dbias, gain, nbias, w_in, b_in, w_out, b_out, lscale = rest[6:16]
    (
    load_sem, pad, gpad, wide, xs, kb, ksum, dgrad, normed_s, gpre_s, hid_s, gout_s,
    packed, pair_recv, merged, mlp_recv, chan_acc, bias_acc, small, small_recv, small_sum, small_all,
    h_send, h_recv, g_send, g_recv, p_send, p_recv, m_send, m_recv, s_send, s_recv, a_send, a_recv, sync,
    ) = rest[16:]
    rows, cols, ch = cot.shape
    hid = w_in.shape[1]
    n_dev = n_lat * n_lon
    lat, lon = lax.axis_index("lat"), lax.axis_index("lon")
    me = lat * n_lon + lon
    per_lat = SMALL_TILES
    first_lon, lon_step = 0, 1

    def where(flat):
        return {"lat": flat // n_lon, "lon": flat % n_lon}

    barrier = pltpu.get_barrier_semaphore()

    def at(dlat, dlon):
        return {"lat": lat + dlat, "lon": (lon + dlon + n_lon) % n_lon}

    for dlat, dlon in DIRS:
        def greet():
            pl.semaphore_signal(barrier, inc=1, device_id=at(dlat, dlon), device_id_type=MESH)

        if dlat:
            pl.when((lat + dlat >= 0) & (lat + dlat < n_lat))(greet)
        else:
            greet()
    rows_beside = jnp.where(lat > 0, 1, 0) + jnp.where(lat < n_lat - 1, 1, 0)

    plane_size = 4 * n_lat - 1
    line_size = n_lon // 4 - 1

    def plane_signal(sem):
        @pl.loop(1, plane_size + 1)
        def _(k):
            place = (lat * 4 + lon % 4 + k) % (plane_size + 1)
            to = {"lat": place // 4, "lon": lon - lon % 4 + place % 4}
            pl.semaphore_signal(sem, inc=1, device_id=to, device_id_type=MESH)

    for k in range(1, line_size + 1):
        pl.semaphore_signal(barrier, inc=1, device_id=at(0, 4 * k), device_id_type=MESH)
    plane_signal(barrier)

    def halo(buf, send, recv, step, which=(-1, 0, 1)):
        cuts = {
            1: ((rows, rows + 3), (0, 3)),
            -1: ((3, 6), (rows + 3, rows + 6)),
            0: ((3, rows + 3), (3, rows + 3)),
        }
        cells = {
            1: ((cols, cols + EDGE), (0, EDGE)),
            -1: ((EDGE, 2 * EDGE), (cols + EDGE, cols + 2 * EDGE)),
            0: ((EDGE, cols + EDGE), (EDGE, cols + EDGE)),
        }
        for d, (dlat, dlon) in enumerate(DIRS):
            if dlat not in which:
                continue
            (s0, s1), (t0, t1) = cuts[dlat]
            (u0, u1), (v0, v1) = cells[dlon]
            copy = pltpu.make_async_remote_copy(
                src_ref=buf.at[pl.ds(s0, s1 - s0), pl.ds(u0, u1 - u0)],
                dst_ref=buf.at[pl.ds(t0, t1 - t0), pl.ds(v0, v1 - v0)],
                send_sem=send.at[d],
                recv_sem=recv.at[d],
                device_id={
                    "lat": lat + dlat,
                    "lon": (lon + dlon + n_lon) % n_lon,
                },
                device_id_type=MESH,
            )
            to = (lat + dlat >= 0) & (lat + dlat < n_lat)
            back = (lat - dlat >= 0) & (lat - dlat < n_lat)
            if step == "start":
                act, cond = copy.start, to
            elif step == "recv":
                act, cond = copy.wait_recv, back
            else:
                act, cond = copy.wait_send, to
            if dlat == 0:
                act()
            else:
                pl.when(cond)(act)

    center = pad.at[pl.ds(3, rows), pl.ds(EDGE, cols)]
    loads = [
        pltpu.make_async_copy(src, dst, load_sem.at[i])
        for i, (src, dst) in enumerate(zip(sources, (center,) + rest[6:16]))
    ]
    for load in loads:
        load.start()

    @pl.when(lat == 0)
    def _():
        pad[0:3] = jnp.zeros((3,) + pad.shape[1:], BF16)
        gpad[0:3] = jnp.zeros((3,) + pad.shape[1:], BF16)

    @pl.when(lat == n_lat - 1)
    def _():
        pad[rows + 3 : rows + 6] = jnp.zeros((3,) + pad.shape[1:], BF16)
        gpad[rows + 3 : rows + 6] = jnp.zeros((3,) + pad.shape[1:], BF16)

    chan_acc[...] = jnp.zeros(chan_acc.shape, F32)
    bias_acc[...] = jnp.zeros(bias_acc.shape, F32)
    small[SMALL_TILES - 1] = jnp.zeros((8, ch), F32)

    loads[0].wait()
    pl.semaphore_wait(barrier, 2 + 3 * rows_beside + line_size + plane_size)
    halo(pad, h_send, h_recv, "start")
    plane_signal(sync)
    for load in loads[1:]:
        load.wait()
    for a in range(7):
        for b in range(7):
            kb[a * 7 + b] = jnp.broadcast_to(dk[a, b : b + 1, :], (8, ch))

    def shifted(buf, start, stop):
        @pl.loop(start, stop)
        def _(r):
            wide[...] = buf[r].astype(F32)
            for b in range(7):
                xs[b, r] = wide[EDGE - 3 + b : EDGE - 3 + b + cols, :]

    def shifted_center(buf):
        @pl.loop(3, rows + 3)
        def _(r):
            wide[EDGE : EDGE + cols, :] = buf[r, EDGE : EDGE + cols, :].astype(F32)
            for b in range(7):
                xs[b, r, 8 : cols - 8, :] = wide[EDGE + 5 + b : EDGE + 5 + b + cols - 16, :]

    def shifted_ends(buf):
        @pl.loop(3, rows + 3)
        def _(r):
            wide[0 : 2 * EDGE, :] = buf[r, 0 : 2 * EDGE, :].astype(F32)
            wide[cols : cols + 2 * EDGE, :] = buf[r, cols : cols + 2 * EDGE, :].astype(F32)
            for b in range(7):
                xs[b, r, 0:8, :] = wide[EDGE - 3 + b : EDGE + 5 + b, :]
                xs[b, r, cols - 8 : cols, :] = wide[cols + EDGE - 11 + b : cols + EDGE - 3 + b, :]

    def chunk(j):
        return pl.ds(pl.multiple_of(j * 8, 8), 8)

    def stencil(j, flip, inputs, acc):
        acc = list(acc)
        for b in range(7):
            taps = [kb[TAPS - 1 - (a * 7 + b) if flip else a * 7 + b] for a in range(7)]
            for r in inputs:
                x = xs[b, r, chunk(j), :]
                for i in range(max(0, r - 6), min(rows, r + 1)):
                    term = taps[r - i] * x
                    acc[i] = term if acc[i] is None else acc[i] + term
        return acc

    inner = range(3, rows + 3)
    chunks = cols // 8
    some = rows // 2
    near = jnp.where(lat == 0, 0, some)
    far = some - near
    ocean = mask[0, 0].astype(F32)

    def whole_rows(j, flip, bias):
        for i, value in enumerate(stencil(j, flip, inner, [None] * rows)):
            dgrad[i, chunk(j), :] = value if bias is None else value + bias[...]

    def center(flip, bias, lo, hi):
        @pl.loop(lo, hi)
        def _(j):
            whole_rows(j, flip, bias)

    def ends_conv(buf, send, recv, flip, bias):
        halo(buf, send, recv, "recv", (0,))
        shifted_ends(buf)

        @pl.loop(0, 2)
        def _(k):
            whole_rows(k * (chunks - 1), flip, bias)

    def sides_conv(buf, send, recv, flip):
        halo(buf, send, recv, "recv", (-1, 1))

        def side(inputs):
            taken = [i for i in range(rows) if any(0 <= r - i < 7 for r in inputs)]
            shifted(buf, inputs[0], inputs[-1] + 1)

            @pl.loop(0, chunks // 2)
            def _(k):
                for j in (2 * k, 2 * k + 1):
                    start = [dgrad[i, chunk(j), :] if i in taken else None for i in range(rows)]
                    values = stencil(j, flip, inputs, start)
                    for i in taken:
                        dgrad[i, chunk(j), :] = values[i]

        pl.when(lat > 0)(functools.partial(side, range(3)))
        pl.when(lat < n_lat - 1)(functools.partial(side, range(rows + 3, rows + 6)))

    shifted_center(pad)
    center(False, dbias, 1, chunks - 1)

    def ends_first():
        ends_conv(pad, h_send, h_recv, False, dbias)

    def sides_first():
        sides_conv(pad, h_send, h_recv, False)

    def when_inside(step):
        if n_lat > 2:
            pl.when((lat > 0) & (lat < n_lat - 1))(step)

    def when_outside(step):
        if n_lat > 2:
            pl.when((lat == 0) | (lat == n_lat - 1))(step)
        else:
            step()

    def mlp(read, write, start, count):
        span = pl.ds(start, count)
        depth = read(dgrad, 0, 0)
        cot_rows = read(cot, 0, 0).astype(F32)
        centered = depth - jnp.sum(depth, axis=-1, keepdims=True) * (1.0 / ch)
        variance = jnp.sum(centered * centered, axis=-1, keepdims=True) * (1.0 / ch)
        inverse = lax.rsqrt(variance + 1e-06)
        normed = centered * inverse
        normed_low = (normed * gain[...] + nbias[...]).astype(BF16)
        pre = jnp.dot(normed_low, w_in[...], preferred_element_type=F32) + b_in[...]
        activated, derivative = gelu_pair(pre)
        hidden_low = activated.astype(BF16)
        out = jnp.dot(hidden_low, w_out[...], preferred_element_type=F32) + b_out[...]
        scaled = ocean * lscale[...]
        write(block_out, 0, 0, (read(pad, 3, EDGE).astype(F32) + scaled * out).astype(BF16))
        grad_out = scaled * cot_rows
        grad_out_low = grad_out.astype(BF16)
        nt = (((1,), (1,)), ((), ()))
        grad_hidden = lax.dot_general(grad_out_low, w_out[...], nt, preferred_element_type=F32)
        grad_pre = grad_hidden * derivative
        grad_pre_low = grad_pre.astype(BF16)
        grad_normed = lax.dot_general(grad_pre_low, w_in[...], nt, preferred_element_type=F32)
        grad_hat = grad_normed * gain[...]
        mean_hat = jnp.sum(grad_hat, axis=-1, keepdims=True) * (1.0 / ch)
        mean_dot = jnp.sum(grad_hat * normed, axis=-1, keepdims=True) * (1.0 / ch)
        grad_depth = inverse * (grad_hat - mean_hat - normed * mean_dot)
        write(dgrad, 0, 0, grad_depth)
        write(gpad, 3, EDGE, grad_depth.astype(BF16))
        normed_s[span, :] = normed_low
        gpre_s[span, :] = grad_pre_low
        hid_s[span, :] = hidden_low
        gout_s[span, :] = grad_out_low
        chan_acc[0] += fold(grad_depth)
        chan_acc[1] += fold(grad_normed * normed)
        chan_acc[2] += fold(grad_normed)
        chan_acc[3] += fold(grad_out)
        chan_acc[4] += fold(ocean * out * cot_rows)
        bias_acc[...] += fold(grad_pre)

    def strip(first, count, lo, hi):
        size = count * (hi - lo)

        def read(buf, above, before):
            return buf[pl.ds(above + first, count), before + lo : before + hi, :].reshape(size, ch)

        def write(buf, above, before, value):
            buf[pl.ds(above + first, count), before + lo : before + hi, :] = value.reshape(count, hi - lo, ch)

        return read, write

    def read_ends(buf, above, before):
        band = pl.ds(above + near, some)
        ends = [buf[band, before + c : before + c + 16, :] for c in (0, cols - 16)]
        return jnp.concatenate([end.reshape(some * 16, ch) for end in ends], axis=0)

    def write_ends(buf, above, before, value):
        band = pl.ds(above + near, some)
        for k, c in enumerate((0, cols - 16)):
            end = value[k * some * 16 : (k + 1) * some * 16]
            buf[band, before + c : before + c + 16, :] = end.reshape(some, 16, ch)

    def kernel_sums(b, first, blocks, sums):
        x, g = [], []
        for k in blocks:
            cells = pl.ds(pl.multiple_of(k * 16, 16), 16)
            x.append([xs[b, first + r, cells, :].astype(BF16) for r in range(some + 6)])
            g.append([dgrad[first + i, cells, :].astype(BF16) for i in range(some)])
        sums = list(sums)
        for a in range(7):
            low = tree([x[k][a + i] * g[k][i] for k in range(len(blocks)) for i in range(some)]).astype(F32)
            sums[a] = sums[a] + (low[0:8] + low[8:16])
        return tuple(sums)

    core = some * (cols - 32)
    ends = some * 32
    when_inside(ends_first)
    when_inside(sides_first)

    mlp(*strip(near, some, 16, cols - 16), 0, core)

    zero = jnp.zeros((8, ch), F32)
    for b in range(7):
        sums = lax.fori_loop(
            0, chunks // 4 - 1, lambda k, sums: kernel_sums(b, near, (2 * k + 1, 2 * k + 2), sums), (zero,) * 7
        )
        for a in range(7):
            ksum[a * 7 + b] = sums[a]

    when_outside(ends_first)
    mlp(read_ends, write_ends, core, ends)
    for b in range(7):
        sums = tuple(ksum[a * 7 + b] for a in range(7))
        sums = kernel_sums(b, near, (0, chunks // 2 - 1), sums)
        for a in range(7):
            ksum[a * 7 + b] = sums[a]
    when_outside(sides_first)

    mlp(*strip(far, some, 0, cols), core + ends, some * cols)

    pl.semaphore_wait(sync, plane_size)

    for b in range(7):
        sums = tuple(ksum[a * 7 + b] for a in range(7))
        sums = lax.fori_loop(
            0, chunks // 4, lambda k, sums: kernel_sums(b, far, (2 * k, 2 * k + 1), sums), sums
        )
        for a in range(7):
            row = a * 7 + b
            small[row // 8, row % 8 : row % 8 + 1, :] = jnp.sum(sums[a], axis=0, keepdims=True)
    for i in range(5):
        row = TAPS + i
        small[row // 8, row % 8 : row % 8 + 1, :] = jnp.sum(chan_acc[i], axis=0, keepdims=True)
    bias_row = jnp.sum(bias_acc[...], axis=0, keepdims=True)
    for i in range(hid // ch):
        row = TAPS + 5 + i
        small[row // 8, row % 8 : row % 8 + 1, :] = bias_row[:, i * ch : (i + 1) * ch]

    def owner_of(t):
        return t // per_lat * n_lon + first_lon + t % per_lat * lon_step

    def small_copy(t):
        owner = owner_of(t)
        return pltpu.make_async_remote_copy(
            src_ref=small.at[t],
            dst_ref=small_recv.at[(owner - me - 1 + n_dev) % n_dev],
            send_sem=s_send.at[t],
            recv_sem=s_recv,
            device_id=where(owner),
            device_id_type=MESH,
        )

    for t in range(SMALL_TILES):

        @pl.when(me != owner_of(t))
        def _():
            small_copy(t).start()

    halo(gpad, g_send, g_recv, "start")

    part = ch // n_lat
    units, half = hid // n_lon, n_lon // 2
    parity = lon % 2
    tt = (((0,), (0,)), ((), ()))
    win_t = lax.dot_general(normed_s[...], gpre_s[...], tt, preferred_element_type=F32).T
    wout_t = lax.dot_general(gout_s[...], hid_s[...], tt, preferred_element_type=F32).T
    lane = lax.broadcasted_iota(jnp.int32, (hid, ch), 1)
    for t in range(n_lat):
        first = pltpu.roll(win_t, (ch - part * t) % ch, 1) if t else win_t
        shift = (part - part * t) % ch
        second = pltpu.roll(wout_t, shift, 1) if shift else wout_t
        both = jnp.where(lane < part, first, second).astype(BF16)
        both = both.reshape(half, 2, units, ch)
        for q in range(2):
            packed[q, t] = both[:, q]

    pair = pltpu.make_async_remote_copy(
        src_ref=packed.at[1 - parity],
        dst_ref=pair_recv,
        send_sem=p_send,
        recv_sem=p_recv,
        device_id={"lat": lat, "lon": lon + 1 - 2 * parity},
        device_id_type=MESH,
    )
    pair.start()

    group = n_lat * half
    mine = lat * half + lon // 2

    def mlp_copy(k):
        to = (mine + 1 + k) % group
        return pltpu.make_async_remote_copy(
            src_ref=merged.at[to // half, to % half],
            dst_ref=mlp_recv.at[k],
            send_sem=m_send,
            recv_sem=m_recv,
            device_id={"lat": to // half, "lon": 2 * (to % half) + parity},
            device_id_type=MESH,
        )

    shifted_center(gpad)
    center(True, None, 1, chunks // 2)
    pair.wait_recv()
    merged[...] = (packed[parity].astype(F32) + pair_recv[...].astype(F32)).astype(BF16)

    @pl.loop(0, group - 1)
    def _(k):
        mlp_copy(k).start()

    center(True, None, chunks // 2, chunks - 1)

    tile = lat * per_lat + (lon - first_lon) // lon_step
    is_owner = (lat < SMALL_TILES // per_lat) & (lon >= first_lon) & (lon < first_lon + per_lat * lon_step)
    is_owner = is_owner & ((lon - first_lon) % lon_step == 0)

    def gather_copy(k):
        to = k + jnp.where(k >= me, 1, 0)
        return pltpu.make_async_remote_copy(
            src_ref=small_sum,
            dst_ref=small_all.at[tile],
            send_sem=a_send,
            recv_sem=a_recv.at[tile],
            device_id=where(to),
            device_id_type=MESH,
        )

    @pl.when(is_owner)
    def _():
        pltpu.make_async_copy(small_recv, small_recv, s_recv).wait()
        total = jnp.sum(small_recv[...], axis=0) + small[tile]
        small_sum[...] = total * scale
        small_all[tile] = total * scale

        @pl.loop(0, n_dev - 1)
        def _(k):
            gather_copy(k).start()

    ends_conv(gpad, g_send, g_recv, True, None)
    sides_conv(gpad, g_send, g_recv, True)

    @pl.loop(0, rows)
    def _(i):
        grad_fields[i] = (cot[i].astype(F32) + dgrad[i]).astype(BF16)

    pltpu.make_async_copy(mlp_recv, mlp_recv, m_recv).wait()
    own = merged[lat, lon // 2].astype(F32)
    total = own + jnp.sum(mlp_recv[...].astype(F32), axis=0)
    total = total * scale
    grad_mlp[0] = total[:, 0:part]
    grad_mlp[1] = total[:, part : 2 * part]

    for t in range(SMALL_TILES):

        @pl.when(me != owner_of(t))
        def _():
            pltpu.make_async_copy(small_sum, small_all.at[t], a_recv.at[t]).wait()

        for k in range(8):
            row, line = t * 8 + k, small_all[t, k : k + 1, :]
            if row < TAPS:
                grad_kernel[row // 7, row % 7 : row % 7 + 1, :] = line
            elif row < TAPS + 5:
                grad_channels[row - TAPS : row - TAPS + 1, :] = line
            elif row < TAPS + 5 + hid // ch:
                first = (row - TAPS - 5) * ch
                grad_bias[:, first : first + ch] = line

    halo(pad, h_send, h_recv, "sent")
    halo(gpad, g_send, g_recv, "sent")
    pair.wait_send()
    pltpu.make_async_copy(mlp_recv, mlp_recv, m_send).wait()
    for t in range(SMALL_TILES):

        @pl.when(me != owner_of(t))
        def _():
            small_copy(t).wait_send()

    @pl.when(is_owner)
    def _():
        pltpu.make_async_copy(small_recv, small_recv, a_send).wait()


def store_kernel(*refs):
    n = len(refs) // 2
    copies = [pltpu.make_async_copy(refs[i], refs[n + i], refs[-1].at[i]) for i in range(n)]
    for copy in copies:
        copy.start()
    for copy in copies:
        copy.wait()


def store(arrays):
    return pl.pallas_call(
        store_kernel,
        out_shape=[pltpu.HBM(x.shape, x.dtype) for x in arrays],
        in_specs=[pl.BlockSpec(memory_space=pltpu.VMEM)] * len(arrays),
        out_specs=[pl.BlockSpec(memory_space=pltpu.HBM)] * len(arrays),
        scratch_shapes=[pltpu.SemaphoreType.DMA((len(arrays),))],
    )(*[pltpu.with_memory_space_constraint(x, pltpu.VMEM) for x in arrays])


def body(mesh_shape, fields, cotangent, ocean_mask, depth_kernel, depth_bias, norm_gain, norm_bias,
         weight_in, bias_in, weight_out, bias_out, layer_scale):
    n_lat, n_lon = mesh_shape
    n_dev = n_lat * n_lon
    rows, cols, ch = fields.shape
    hid = weight_in.shape[1]
    units, part, cells = hid // n_lon, ch // n_lat, rows * cols
    scale = 1.0 / math.sqrt(cells * n_dev)
    vmem = pl.BlockSpec(memory_space=pltpu.VMEM)
    shares = (n_lat, n_lon // 2, units, ch)
    padded = (rows + 6, cols + 2 * EDGE, ch)
    operands = (
        fields, cotangent, depth_kernel, depth_bias.reshape(1, ch), norm_gain.reshape(1, ch),
        norm_bias.reshape(1, ch), weight_in, bias_in.reshape(1, hid), weight_out,
        bias_out.reshape(1, ch), layer_scale.reshape(1, ch),
    )
    outs = pl.pallas_call(
        functools.partial(kernel, n_lat, n_lon, scale),
        out_shape=[
            jax.ShapeDtypeStruct(fields.shape, BF16),
            jax.ShapeDtypeStruct(fields.shape, BF16),
            jax.ShapeDtypeStruct((2, units, part), F32),
            jax.ShapeDtypeStruct((7, 7, ch), F32),
            jax.ShapeDtypeStruct((5, ch), F32),
            jax.ShapeDtypeStruct((1, hid), F32),
        ],
        in_specs=[pl.BlockSpec(memory_space=pltpu.SMEM)] + [pl.BlockSpec(memory_space=pltpu.HBM)] * 11,
        out_specs=[vmem] * 6,
        scratch_shapes=[pltpu.VMEM(x.shape, x.dtype) for x in operands[1:]]
        + [
            pltpu.SemaphoreType.DMA((11,)),
            pltpu.VMEM(padded, BF16),
            pltpu.VMEM(padded, BF16),
            pltpu.VMEM(padded[1:], F32),
            pltpu.VMEM((7, rows + 6, cols, ch), F32),
            pltpu.VMEM((TAPS, 8, ch), F32),
            pltpu.VMEM((TAPS, 8, ch), F32),
            pltpu.VMEM((rows, cols, ch), F32),
            pltpu.VMEM((cells, ch), BF16),
            pltpu.VMEM((cells, hid), BF16),
            pltpu.VMEM((cells, hid), BF16),
            pltpu.VMEM((cells, ch), BF16),
            pltpu.VMEM((2,) + shares, BF16),
            pltpu.VMEM(shares, BF16),
            pltpu.VMEM(shares, BF16),
            pltpu.VMEM((n_dev // 2 - 1, units, ch), BF16),
            pltpu.VMEM((5, 8, ch), F32),
            pltpu.VMEM((8, hid), F32),
            pltpu.VMEM((SMALL_TILES, 8, ch), F32),
            pltpu.VMEM((n_dev - 1, 8, ch), F32),
            pltpu.VMEM((8, ch), F32),
            pltpu.VMEM((SMALL_TILES, 8, ch), F32),
            pltpu.SemaphoreType.DMA((8,)),
            pltpu.SemaphoreType.DMA((8,)),
            pltpu.SemaphoreType.DMA((8,)),
            pltpu.SemaphoreType.DMA((8,)),
            pltpu.SemaphoreType.DMA,
            pltpu.SemaphoreType.DMA,
            pltpu.SemaphoreType.DMA,
            pltpu.SemaphoreType.DMA,
            pltpu.SemaphoreType.DMA((SMALL_TILES,)),
            pltpu.SemaphoreType.DMA,
            pltpu.SemaphoreType.DMA,
            pltpu.SemaphoreType.DMA((SMALL_TILES,)),
            pltpu.SemaphoreType.REGULAR,
        ],
        compiler_params=pltpu.CompilerParams(
            collective_id=0, has_side_effects=True, vmem_limit_bytes=48 << 20
        ),
    )(ocean_mask, *[pltpu.with_memory_space_constraint(x, pltpu.HBM) for x in operands])
    outs = store(outs)
    return (outs[0], outs[1], outs[2].transpose(0, 2, 1), outs[3], outs[4], outs[5].reshape(hid))


def solution(mesh):
    tiled = P("lat", "lon", None)
    placed = (tiled, tiled, P("lat", "lon")) + (P(),) * 9
    return jax.shard_map(
        functools.partial(body, (mesh.shape["lat"], mesh.shape["lon"])),
        mesh=mesh,
        in_specs=placed,
        out_specs=(tiled, tiled, P(None, "lat", "lon"), P(), P(), P()),
        check_vma=False,
    )
```

```python
import functools
import math

import jax
import jax.numpy as jnp
from jax import lax
from jax.experimental import pallas as pl
from jax.experimental.pallas import tpu as pltpu
from jax.sharding import PartitionSpec as P

GELU_COEF = 0.7978845608028654
MESH = pl.DeviceIdType.MESH
F32 = jnp.float32
BF16 = jnp.bfloat16
EDGE = 16
DIRS = [(a, b) for a in (-1, 0, 1) for b in (-1, 0, 1) if (a, b) != (0, 0)]
TAPS = 49
SMALL_TILES = 8


def gelu_pair(v):
    sq = v * v
    half = 0.5 + 0.5 * jnp.tanh(v * (GELU_COEF + (0.044715 * GELU_COEF) * sq))
    activated = v * half
    slope = (1.0 - half) * (2.0 * GELU_COEF + (6.0 * 0.044715 * GELU_COEF) * sq)
    return activated, half + activated * slope


def fold(x):
    return jnp.sum(x.reshape(x.shape[0] // 8, 8, x.shape[1]), axis=0)


def tree(terms):
    while len(terms) > 1:
        pairs = [terms[k] + terms[k + 1] for k in range(0, len(terms) - 1, 2)]
        terms = pairs + terms[len(terms) - len(terms) % 2 :]
    return terms[0]


def kernel(
    n_lat, n_lon, scale,
    mask, fields_hbm, *rest,
):
    sources, rest = (fields_hbm,) + rest[:10], rest[10:]
    block_out, grad_fields, grad_mlp, grad_kernel, grad_channels, grad_bias = rest[:6]
    cot, dk, dbias, gain, nbias, w_in, b_in, w_out, b_out, lscale = rest[6:16]
    (
    load_sem, pad, gpad, wide, xs, kb, ksum, dgrad, normed_s, gpre_s, hid_s, gout_s,
    packed, pair_recv, merged, mlp_recv, chan_acc, bias_acc, small, small_recv, small_sum, small_all,
    h_send, h_recv, g_send, g_recv, p_send, p_recv, m_send, m_recv, s_send, s_recv, a_send, a_recv, sync,
    ) = rest[16:]
    rows, cols, ch = cot.shape
    hid = w_in.shape[1]
    n_dev = n_lat * n_lon
    lat, lon = lax.axis_index("lat"), lax.axis_index("lon")
    me = lat * n_lon + lon
    per_lat = SMALL_TILES
    first_lon, lon_step = 0, 1

    def where(flat):
        return {"lat": flat // n_lon, "lon": flat % n_lon}

    barrier = pltpu.get_barrier_semaphore()

    def at(dlat, dlon):
        return {"lat": lat + dlat, "lon": (lon + dlon + n_lon) % n_lon}

    for dlat, dlon in DIRS:
        def greet():
            pl.semaphore_signal(barrier, inc=1, device_id=at(dlat, dlon), device_id_type=MESH)

        if dlat:
            pl.when((lat + dlat >= 0) & (lat + dlat < n_lat))(greet)
        else:
            greet()
    rows_beside = jnp.where(lat > 0, 1, 0) + jnp.where(lat < n_lat - 1, 1, 0)

    plane_size = 4 * n_lat - 1
    line_size = n_lon // 4 - 1

    def plane_signal(sem):
        @pl.loop(1, plane_size + 1)
        def _(k):
            place = (lat * 4 + lon % 4 + k) % (plane_size + 1)
            to = {"lat": place // 4, "lon": lon - lon % 4 + place % 4}
            pl.semaphore_signal(sem, inc=1, device_id=to, device_id_type=MESH)

    for k in range(1, line_size + 1):
        pl.semaphore_signal(barrier, inc=1, device_id=at(0, 4 * k), device_id_type=MESH)
    plane_signal(barrier)

    def halo(buf, send, recv, step, which=(-1, 0, 1)):
        cuts = {
            1: ((rows, rows + 3), (0, 3)),
            -1: ((3, 6), (rows + 3, rows + 6)),
            0: ((3, rows + 3), (3, rows + 3)),
        }
        cells = {
            1: ((cols, cols + EDGE), (0, EDGE)),
            -1: ((EDGE, 2 * EDGE), (cols + EDGE, cols + 2 * EDGE)),
            0: ((EDGE, cols + EDGE), (EDGE, cols + EDGE)),
        }
        for d, (dlat, dlon) in enumerate(DIRS):
            if dlat not in which:
                continue
            (s0, s1), (t0, t1) = cuts[dlat]
            (u0, u1), (v0, v1) = cells[dlon]
            copy = pltpu.make_async_remote_copy(
                src_ref=buf.at[pl.ds(s0, s1 - s0), pl.ds(u0, u1 - u0)],
                dst_ref=buf.at[pl.ds(t0, t1 - t0), pl.ds(v0, v1 - v0)],
                send_sem=send.at[d],
                recv_sem=recv.at[d],
                device_id={
                    "lat": lat + dlat,
                    "lon": (lon + dlon + n_lon) % n_lon,
                },
                device_id_type=MESH,
            )
            to = (lat + dlat >= 0) & (lat + dlat < n_lat)
            back = (lat - dlat >= 0) & (lat - dlat < n_lat)
            if step == "start":
                act, cond = copy.start, to
            elif step == "recv":
                act, cond = copy.wait_recv, back
            else:
                act, cond = copy.wait_send, to
            if dlat == 0:
                act()
            else:
                pl.when(cond)(act)

    center = pad.at[pl.ds(3, rows), pl.ds(EDGE, cols)]
    loads = [
        pltpu.make_async_copy(src, dst, load_sem.at[i])
        for i, (src, dst) in enumerate(zip(sources, (center,) + rest[6:16]))
    ]
    for load in loads:
        load.start()

    @pl.when(lat == 0)
    def _():
        pad[0:3] = jnp.zeros((3,) + pad.shape[1:], BF16)
        gpad[0:3] = jnp.zeros((3,) + pad.shape[1:], BF16)

    @pl.when(lat == n_lat - 1)
    def _():
        pad[rows + 3 : rows + 6] = jnp.zeros((3,) + pad.shape[1:], BF16)
        gpad[rows + 3 : rows + 6] = jnp.zeros((3,) + pad.shape[1:], BF16)

    chan_acc[...] = jnp.zeros(chan_acc.shape, F32)
    bias_acc[...] = jnp.zeros(bias_acc.shape, F32)
    small[SMALL_TILES - 1] = jnp.zeros((8, ch), F32)

    loads[0].wait()
    pl.semaphore_wait(barrier, 2 + 3 * rows_beside + line_size + plane_size)
    halo(pad, h_send, h_recv, "start")
    plane_signal(sync)
    for load in loads[1:]:
        load.wait()
    for a in range(7):
        for b in range(7):
            kb[a * 7 + b] = jnp.broadcast_to(dk[a, b : b + 1, :], (8, ch))

    def shifted(buf, start, stop):
        @pl.loop(start, stop)
        def _(r):
            wide[...] = buf[r].astype(F32)
            for b in range(7):
                xs[b, r] = wide[EDGE - 3 + b : EDGE - 3 + b + cols, :]

    def shifted_center(buf):
        @pl.loop(3, rows + 3)
        def _(r):
            wide[EDGE : EDGE + cols, :] = buf[r, EDGE : EDGE + cols, :].astype(F32)
            for b in range(7):
                xs[b, r, 8 : cols - 8, :] = wide[EDGE + 5 + b : EDGE + 5 + b + cols - 16, :]

    def shifted_ends(buf):
        @pl.loop(3, rows + 3)
        def _(r):
            wide[0 : 2 * EDGE, :] = buf[r, 0 : 2 * EDGE, :].astype(F32)
            wide[cols : cols + 2 * EDGE, :] = buf[r, cols : cols + 2 * EDGE, :].astype(F32)
            for b in range(7):
                xs[b, r, 0:8, :] = wide[EDGE - 3 + b : EDGE + 5 + b, :]
                xs[b, r, cols - 8 : cols, :] = wide[cols + EDGE - 11 + b : cols + EDGE - 3 + b, :]

    def chunk(j):
        return pl.ds(pl.multiple_of(j * 8, 8), 8)

    def stencil(j, flip, inputs, acc):
        acc = list(acc)
        for b in range(7):
            taps = [kb[TAPS - 1 - (a * 7 + b) if flip else a * 7 + b] for a in range(7)]
            for r in inputs:
                x = xs[b, r, chunk(j), :]
                for i in range(max(0, r - 6), min(rows, r + 1)):
                    term = taps[r - i] * x
                    acc[i] = term if acc[i] is None else acc[i] + term
        return acc

    inner = range(3, rows + 3)
    chunks = cols // 8
    some = rows // 2
    near = jnp.where(lat == 0, 0, some)
    far = some - near
    ocean = mask[0, 0].astype(F32)

    def whole_rows(j, flip, bias):
        for i, value in enumerate(stencil(j, flip, inner, [None] * rows)):
            dgrad[i, chunk(j), :] = value if bias is None else value + bias[...]

    def center(flip, bias, lo, hi):
        @pl.loop(lo, hi)
        def _(j):
            whole_rows(j, flip, bias)

    def ends_conv(buf, send, recv, flip, bias):
        halo(buf, send, recv, "recv", (0,))
        shifted_ends(buf)

        @pl.loop(0, 2)
        def _(k):
            whole_rows(k * (chunks - 1), flip, bias)

    def sides_conv(buf, send, recv, flip):
        halo(buf, send, recv, "recv", (-1, 1))

        def side(inputs):
            taken = [i for i in range(rows) if any(0 <= r - i < 7 for r in inputs)]
            shifted(buf, inputs[0], inputs[-1] + 1)

            @pl.loop(0, chunks // 2)
            def _(k):
                for j in (2 * k, 2 * k + 1):
                    start = [dgrad[i, chunk(j), :] if i in taken else None for i in range(rows)]
                    values = stencil(j, flip, inputs, start)
                    for i in taken:
                        dgrad[i, chunk(j), :] = values[i]

        pl.when(lat > 0)(functools.partial(side, range(3)))
        pl.when(lat < n_lat - 1)(functools.partial(side, range(rows + 3, rows + 6)))

    shifted_center(pad)
    center(False, dbias, 1, chunks - 1)

    def ends_first():
        ends_conv(pad, h_send, h_recv, False, dbias)

    def sides_first():
        sides_conv(pad, h_send, h_recv, False)

    def when_inside(step):
        if n_lat > 2:
            pl.when((lat > 0) & (lat < n_lat - 1))(step)

    def when_outside(step):
        if n_lat > 2:
            pl.when((lat == 0) | (lat == n_lat - 1))(step)
        else:
            step()

    def mlp(read, write, start, count):
        span = pl.ds(start, count)
        depth = read(dgrad, 0, 0)
        cot_rows = read(cot, 0, 0).astype(F32)
        centered = depth - jnp.sum(depth, axis=-1, keepdims=True) * (1.0 / ch)
        variance = jnp.sum(centered * centered, axis=-1, keepdims=True) * (1.0 / ch)
        inverse = lax.rsqrt(variance + 1e-06)
        normed = centered * inverse
        normed_low = (normed * gain[...] + nbias[...]).astype(BF16)
        pre = jnp.dot(normed_low, w_in[...], preferred_element_type=F32) + b_in[...]
        activated, derivative = gelu_pair(pre)
        hidden_low = activated.astype(BF16)
        out = jnp.dot(hidden_low, w_out[...], preferred_element_type=F32) + b_out[...]
        scaled = ocean * lscale[...]
        write(block_out, 0, 0, (read(pad, 3, EDGE).astype(F32) + scaled * out).astype(BF16))
        grad_out = scaled * cot_rows
        grad_out_low = grad_out.astype(BF16)
        nt = (((1,), (1,)), ((), ()))
        grad_hidden = lax.dot_general(grad_out_low, w_out[...], nt, preferred_element_type=F32)
        grad_pre = grad_hidden * derivative
        grad_pre_low = grad_pre.astype(BF16)
        grad_normed = lax.dot_general(grad_pre_low, w_in[...], nt, preferred_element_type=F32)
        grad_hat = grad_normed * gain[...]
        mean_hat = jnp.sum(grad_hat, axis=-1, keepdims=True) * (1.0 / ch)
        mean_dot = jnp.sum(grad_hat * normed, axis=-1, keepdims=True) * (1.0 / ch)
        grad_depth = inverse * (grad_hat - mean_hat - normed * mean_dot)
        write(dgrad, 0, 0, grad_depth)
        write(gpad, 3, EDGE, grad_depth.astype(BF16))
        normed_s[span, :] = normed_low
        gpre_s[span, :] = grad_pre_low
        hid_s[span, :] = hidden_low
        gout_s[span, :] = grad_out_low
        chan_acc[0] += fold(grad_depth)
        chan_acc[1] += fold(grad_normed * normed)
        chan_acc[2] += fold(grad_normed)
        chan_acc[3] += fold(grad_out)
        chan_acc[4] += fold(ocean * out * cot_rows)
        bias_acc[...] += fold(grad_pre)

    def strip(first, count, lo, hi):
        size = count * (hi - lo)

        def read(buf, above, before):
            return buf[pl.ds(above + first, count), before + lo : before + hi, :].reshape(size, ch)

        def write(buf, above, before, value):
            buf[pl.ds(above + first, count), before + lo : before + hi, :] = value.reshape(count, hi - lo, ch)

        return read, write

    def read_ends(buf, above, before):
        band = pl.ds(above + near, some)
        ends = [buf[band, before + c : before + c + 16, :] for c in (0, cols - 16)]
        return jnp.concatenate([end.reshape(some * 16, ch) for end in ends], axis=0)

    def write_ends(buf, above, before, value):
        band = pl.ds(above + near, some)
        for k, c in enumerate((0, cols - 16)):
            end = value[k * some * 16 : (k + 1) * some * 16]
            buf[band, before + c : before + c + 16, :] = end.reshape(some, 16, ch)

    def kernel_sums(b, first, blocks, sums):
        x, g = [], []
        for k in blocks:
            cells = pl.ds(pl.multiple_of(k * 16, 16), 16)
            x.append([xs[b, first + r, cells, :].astype(BF16) for r in range(some + 6)])
            g.append([dgrad[first + i, cells, :].astype(BF16) for i in range(some)])
        sums = list(sums)
        for a in range(7):
            low = tree([x[k][a + i] * g[k][i] for k in range(len(blocks)) for i in range(some)]).astype(F32)
            sums[a] = sums[a] + (low[0:8] + low[8:16])
        return tuple(sums)

    core = some * (cols - 32)
    ends = some * 32
    when_inside(ends_first)
    when_inside(sides_first)

    mlp(*strip(near, some, 16, cols - 16), 0, core)

    zero = jnp.zeros((8, ch), F32)
    for b in range(7):
        sums = lax.fori_loop(
            0, chunks // 4 - 1, lambda k, sums: kernel_sums(b, near, (2 * k + 1, 2 * k + 2), sums), (zero,) * 7
        )
        for a in range(7):
            ksum[a * 7 + b] = sums[a]

    when_outside(ends_first)
    mlp(read_ends, write_ends, core, ends)
    for b in range(7):
        sums = tuple(ksum[a * 7 + b] for a in range(7))
        sums = kernel_sums(b, near, (0, chunks // 2 - 1), sums)
        for a in range(7):
            ksum[a * 7 + b] = sums[a]
    when_outside(sides_first)

    mlp(*strip(far, some, 0, cols), core + ends, some * cols)

    pl.semaphore_wait(sync, plane_size)

    for b in range(7):
        sums = tuple(ksum[a * 7 + b] for a in range(7))
        sums = lax.fori_loop(
            0,
            chunks // 8,
            lambda k, sums: kernel_sums(
                b, far, (4 * k + 2, 4 * k + 3), kernel_sums(b, far, (4 * k, 4 * k + 1), sums)
            ),
            sums,
        )
        for a in range(7):
            row = a * 7 + b
            small[row // 8, row % 8 : row % 8 + 1, :] = jnp.sum(sums[a], axis=0, keepdims=True)
    for i in range(5):
        row = TAPS + i
        small[row // 8, row % 8 : row % 8 + 1, :] = jnp.sum(chan_acc[i], axis=0, keepdims=True)
    bias_row = jnp.sum(bias_acc[...], axis=0, keepdims=True)
    for i in range(hid // ch):
        row = TAPS + 5 + i
        small[row // 8, row % 8 : row % 8 + 1, :] = bias_row[:, i * ch : (i + 1) * ch]

    def owner_of(t):
        return t // per_lat * n_lon + first_lon + t % per_lat * lon_step

    def small_copy(t):
        owner = owner_of(t)
        return pltpu.make_async_remote_copy(
            src_ref=small.at[t],
            dst_ref=small_recv.at[(owner - me - 1 + n_dev) % n_dev],
            send_sem=s_send.at[t],
            recv_sem=s_recv,
            device_id=where(owner),
            device_id_type=MESH,
        )

    for t in range(SMALL_TILES):

        @pl.when(me != owner_of(t))
        def _():
            small_copy(t).start()

    halo(gpad, g_send, g_recv, "start")

    part = ch // n_lat
    units, half = hid // n_lon, n_lon // 2
    parity = lon % 2
    tt = (((0,), (0,)), ((), ()))
    win_t = lax.dot_general(normed_s[...], gpre_s[...], tt, preferred_element_type=F32).T
    wout_t = lax.dot_general(gout_s[...], hid_s[...], tt, preferred_element_type=F32).T
    lane = lax.broadcasted_iota(jnp.int32, (hid, ch), 1)
    for t in range(n_lat):
        first = pltpu.roll(win_t, (ch - part * t) % ch, 1) if t else win_t
        shift = (part - part * t) % ch
        second = pltpu.roll(wout_t, shift, 1) if shift else wout_t
        both = jnp.where(lane < part, first, second).astype(BF16)
        both = both.reshape(half, 2, units, ch)
        for q in range(2):
            packed[q, t] = both[:, q]

    pair = pltpu.make_async_remote_copy(
        src_ref=packed.at[1 - parity],
        dst_ref=pair_recv,
        send_sem=p_send,
        recv_sem=p_recv,
        device_id={"lat": lat, "lon": lon + 1 - 2 * parity},
        device_id_type=MESH,
    )
    pair.start()

    group = n_lat * half
    mine = lat * half + lon // 2

    def mlp_copy(k):
        to = (mine + 1 + k) % group
        return pltpu.make_async_remote_copy(
            src_ref=merged.at[to // half, to % half],
            dst_ref=mlp_recv.at[k],
            send_sem=m_send,
            recv_sem=m_recv,
            device_id={"lat": to // half, "lon": 2 * (to % half) + parity},
            device_id_type=MESH,
        )

    shifted_center(gpad)
    center(True, None, 1, chunks // 2)
    pair.wait_recv()
    merged[...] = (packed[parity].astype(F32) + pair_recv[...].astype(F32)).astype(BF16)

    @pl.loop(0, group - 1)
    def _(k):
        mlp_copy(k).start()

    center(True, None, chunks // 2, chunks - 1)

    tile = lat * per_lat + (lon - first_lon) // lon_step
    is_owner = (lat < SMALL_TILES // per_lat) & (lon >= first_lon) & (lon < first_lon + per_lat * lon_step)
    is_owner = is_owner & ((lon - first_lon) % lon_step == 0)

    def gather_copy(k):
        to = k + jnp.where(k >= me, 1, 0)
        return pltpu.make_async_remote_copy(
            src_ref=small_sum,
            dst_ref=small_all.at[tile],
            send_sem=a_send,
            recv_sem=a_recv.at[tile],
            device_id=where(to),
            device_id_type=MESH,
        )

    @pl.when(is_owner)
    def _():
        pltpu.make_async_copy(small_recv, small_recv, s_recv).wait()
        total = jnp.sum(small_recv[...], axis=0) + small[tile]
        small_sum[...] = total * scale
        small_all[tile] = total * scale

        @pl.loop(0, n_dev - 1)
        def _(k):
            gather_copy(k).start()

    ends_conv(gpad, g_send, g_recv, True, None)
    sides_conv(gpad, g_send, g_recv, True)

    @pl.loop(0, rows)
    def _(i):
        grad_fields[i] = (cot[i].astype(F32) + dgrad[i]).astype(BF16)

    pltpu.make_async_copy(mlp_recv, mlp_recv, m_recv).wait()
    own = merged[lat, lon // 2].astype(F32)
    total = own + jnp.sum(mlp_recv[...].astype(F32), axis=0)
    total = total * scale
    grad_mlp[0] = total[:, 0:part]
    grad_mlp[1] = total[:, part : 2 * part]

    for t in range(SMALL_TILES):

        @pl.when(me != owner_of(t))
        def _():
            pltpu.make_async_copy(small_sum, small_all.at[t], a_recv.at[t]).wait()

        for k in range(8):
            row, line = t * 8 + k, small_all[t, k : k + 1, :]
            if row < TAPS:
                grad_kernel[row // 7, row % 7 : row % 7 + 1, :] = line
            elif row < TAPS + 5:
                grad_channels[row - TAPS : row - TAPS + 1, :] = line
            elif row < TAPS + 5 + hid // ch:
                first = (row - TAPS - 5) * ch
                grad_bias[:, first : first + ch] = line

    halo(pad, h_send, h_recv, "sent")
    halo(gpad, g_send, g_recv, "sent")
    pair.wait_send()
    pltpu.make_async_copy(mlp_recv, mlp_recv, m_send).wait()
    for t in range(SMALL_TILES):

        @pl.when(me != owner_of(t))
        def _():
            small_copy(t).wait_send()

    @pl.when(is_owner)
    def _():
        pltpu.make_async_copy(small_recv, small_recv, a_send).wait()


def store_kernel(*refs):
    n = len(refs) // 2
    copies = [pltpu.make_async_copy(refs[i], refs[n + i], refs[-1].at[i]) for i in range(n)]
    for copy in copies:
        copy.start()
    for copy in copies:
        copy.wait()


def store(arrays):
    return pl.pallas_call(
        store_kernel,
        out_shape=[pltpu.HBM(x.shape, x.dtype) for x in arrays],
        in_specs=[pl.BlockSpec(memory_space=pltpu.VMEM)] * len(arrays),
        out_specs=[pl.BlockSpec(memory_space=pltpu.HBM)] * len(arrays),
        scratch_shapes=[pltpu.SemaphoreType.DMA((len(arrays),))],
    )(*[pltpu.with_memory_space_constraint(x, pltpu.VMEM) for x in arrays])


def body(mesh_shape, fields, cotangent, ocean_mask, depth_kernel, depth_bias, norm_gain, norm_bias,
         weight_in, bias_in, weight_out, bias_out, layer_scale):
    n_lat, n_lon = mesh_shape
    n_dev = n_lat * n_lon
    rows, cols, ch = fields.shape
    hid = weight_in.shape[1]
    units, part, cells = hid // n_lon, ch // n_lat, rows * cols
    scale = 1.0 / math.sqrt(cells * n_dev)
    vmem = pl.BlockSpec(memory_space=pltpu.VMEM)
    shares = (n_lat, n_lon // 2, units, ch)
    padded = (rows + 6, cols + 2 * EDGE, ch)
    operands = (
        fields, cotangent, depth_kernel, depth_bias.reshape(1, ch), norm_gain.reshape(1, ch),
        norm_bias.reshape(1, ch), weight_in, bias_in.reshape(1, hid), weight_out,
        bias_out.reshape(1, ch), layer_scale.reshape(1, ch),
    )
    outs = pl.pallas_call(
        functools.partial(kernel, n_lat, n_lon, scale),
        out_shape=[
            jax.ShapeDtypeStruct(fields.shape, BF16),
            jax.ShapeDtypeStruct(fields.shape, BF16),
            jax.ShapeDtypeStruct((2, units, part), F32),
            jax.ShapeDtypeStruct((7, 7, ch), F32),
            jax.ShapeDtypeStruct((5, ch), F32),
            jax.ShapeDtypeStruct((1, hid), F32),
        ],
        in_specs=[pl.BlockSpec(memory_space=pltpu.SMEM)] + [pl.BlockSpec(memory_space=pltpu.HBM)] * 11,
        out_specs=[vmem] * 6,
        scratch_shapes=[pltpu.VMEM(x.shape, x.dtype) for x in operands[1:]]
        + [
            pltpu.SemaphoreType.DMA((11,)),
            pltpu.VMEM(padded, BF16),
            pltpu.VMEM(padded, BF16),
            pltpu.VMEM(padded[1:], F32),
            pltpu.VMEM((7, rows + 6, cols, ch), F32),
            pltpu.VMEM((TAPS, 8, ch), F32),
            pltpu.VMEM((TAPS, 8, ch), F32),
            pltpu.VMEM((rows, cols, ch), F32),
            pltpu.VMEM((cells, ch), BF16),
            pltpu.VMEM((cells, hid), BF16),
            pltpu.VMEM((cells, hid), BF16),
            pltpu.VMEM((cells, ch), BF16),
            pltpu.VMEM((2,) + shares, BF16),
            pltpu.VMEM(shares, BF16),
            pltpu.VMEM(shares, BF16),
            pltpu.VMEM((n_dev // 2 - 1, units, ch), BF16),
            pltpu.VMEM((5, 8, ch), F32),
            pltpu.VMEM((8, hid), F32),
            pltpu.VMEM((SMALL_TILES, 8, ch), F32),
            pltpu.VMEM((n_dev - 1, 8, ch), F32),
            pltpu.VMEM((8, ch), F32),
            pltpu.VMEM((SMALL_TILES, 8, ch), F32),
            pltpu.SemaphoreType.DMA((8,)),
            pltpu.SemaphoreType.DMA((8,)),
            pltpu.SemaphoreType.DMA((8,)),
            pltpu.SemaphoreType.DMA((8,)),
            pltpu.SemaphoreType.DMA,
            pltpu.SemaphoreType.DMA,
            pltpu.SemaphoreType.DMA,
            pltpu.SemaphoreType.DMA,
            pltpu.SemaphoreType.DMA((SMALL_TILES,)),
            pltpu.SemaphoreType.DMA,
            pltpu.SemaphoreType.DMA,
            pltpu.SemaphoreType.DMA((SMALL_TILES,)),
            pltpu.SemaphoreType.REGULAR,
        ],
        compiler_params=pltpu.CompilerParams(
            collective_id=0, has_side_effects=True, vmem_limit_bytes=48 << 20
        ),
    )(ocean_mask, *[pltpu.with_memory_space_constraint(x, pltpu.HBM) for x in operands])
    outs = store(outs)
    return (outs[0], outs[1], outs[2].transpose(0, 2, 1), outs[3], outs[4], outs[5].reshape(hid))


def solution(mesh):
    tiled = P("lat", "lon", None)
    placed = (tiled, tiled, P("lat", "lon")) + (P(),) * 9
    return jax.shard_map(
        functools.partial(body, (mesh.shape["lat"], mesh.shape["lon"])),
        mesh=mesh,
        in_specs=placed,
        out_specs=(tiled, tiled, P(None, "lat", "lon"), P(), P(), P()),
        check_vma=False,
    )
```
